32 devices in a mesh: prow: 4 (over y, x), pcol: 8 (over z, core).
Axes of the slice: x: 2, y: 2, z: 4, core: 2. Of those that a mesh axis runs over, the one named last changes fastest.
Arguments:
- l_panel: bfloat16 [8192, 1024], P('prow', 'pcol'), may hold values from -0.29882812 to 0.29882812
- inverse_tile: bfloat16 [8192, 8192], P('prow', 'pcol'), may hold values from -0.5 to 0.5
- unit_inverse: bfloat16 [8, 128, 128], P('pcol'), may hold values from -0.5 to 0.5
- pivot_inverse: float32 [8, 128, 128], P('pcol'), may hold values from -6 to 6
- listed: int32 [8, 64], replicated, may hold values 0 or 1
Outputs:
- offdiag: float32 [1024, 8192], P('pcol', 'prow')
- diag: float32 [8, 128, 128], P('pcol')
The draws below stay inside these ranges and needn't reach their ends.
All inputs are finite; a program needn't handle non-finite values.
Results may differ from the reference program's by a relative error of at most 0.015.
Values may be sent and summed in bfloat16 or wider, within the bound.
No kernel may reach another device: no remote copies, remote signals or barrier semaphores. Data moves between devices by JAX's collectives and lax.ppermute only.
A program may use at most 64 MiB of HBM per device.

```python
import jax
import jax.numpy as jnp
from jax import lax

W = 128
BLOCK = 128
S = 8
NBLK = 64
NA = 8192
N_PCOL = 8


def plant(values, key, least, top_value):
    longest = values.shape.index(max(values.shape))
    spots = []
    for shift in (0, 1):
        where = [jax.random.randint(jax.random.fold_in(key, axis), (), 0, length) for axis, length in enumerate(values.shape)]
        where[longest] = (where[longest] + shift) % values.shape[longest]
        spots.append(tuple(where))
    return values.at[spots[0]].set(least).at[spots[1]].set(top_value)


def block_levels(key, extent, shards, smallest, high):
    def one(axis_at, shards_of):
        draws = jax.random.uniform(jax.random.fold_in(jax.random.fold_in(key, 6), axis_at), (shards_of,), jnp.float32, smallest / len(shards), high / len(shards))
        return jnp.repeat(jnp.exp(draws), extent[axis_at] // shards_of).reshape((-1,) + (1,) * (len(extent) - axis_at - 1))

    loudness = one(*shards[0])
    for cut in shards[1:]:
        loudness = loudness * one(*cut)
    return loudness


def gaussian(stream_key, shape, deviation, bound, shards=(), held_as=jnp.bfloat16):
    values = deviation * jax.random.normal(stream_key, shape, jnp.float32)
    if shards:
        values = values * block_levels(stream_key, shape, shards, -0.22, 0.18)
    return jnp.clip(values, -bound, bound).astype(held_as)


def setup_inputs(seed: int = 0) -> dict:
    splits = jax.random.split(jax.random.key(seed), 6)
    l_panel = gaussian(splits[0], (NA, S * W), 0.05, 0.29882812, ((0, 4), (1, 8)))
    inverse_tile = gaussian(splits[1], (NA, NA), (NA // 64) ** -0.5, 0.5, ((0, 4), (1, 8)))
    unit_inverse = gaussian(splits[2], (S, W, W), W ** -0.5, 0.5, ((0, 8),))
    pivot_inverse = gaussian(splits[3], (S, W, W), 1.0, 6.0, ((0, 8),), jnp.float32)
    listed = plant((jax.random.randint(splits[4], (S, NBLK), 0, 4) < 3).astype(jnp.int32), jax.random.fold_in(splits[4], 1), 0, 1)
    return {"l_panel": l_panel, "inverse_tile": inverse_tile, "unit_inverse": unit_inverse, "pivot_inverse": pivot_inverse, "listed": listed}


def reference(l_panel, inverse_tile, unit_inverse, pivot_inverse, listed):
    row_mask = jnp.repeat(listed, BLOCK, axis=1).astype(jnp.float32)
    panel = l_panel.reshape(NA, S, W).astype(jnp.float32)
    masked = (panel * row_mask.T[:, :, None]).astype(jnp.bfloat16)
    lhat = jnp.einsum("nsw,swv->nsv", masked.astype(jnp.float32), unit_inverse.astype(jnp.float32), precision=lax.Precision.HIGHEST).astype(jnp.bfloat16)
    lhat_flat = lhat.reshape(NA, S * W)
    span = NA // N_PCOL

    def add_range(total, index):
        start = (index * span).astype(jnp.int32)
        cols = lax.dynamic_slice_in_dim(inverse_tile, start, span, 1)
        rows_part = lax.dynamic_slice_in_dim(lhat_flat, start, span, 0)
        partial_value = jnp.dot(cols, rows_part, preferred_element_type=jnp.float32).astype(jnp.bfloat16)
        return total + partial_value.astype(jnp.float32), None

    product, unused = lax.scan(add_range, jnp.zeros((NA, S * W), jnp.float32), jnp.arange(N_PCOL, dtype=jnp.int32))
    wide_mask = jnp.repeat(row_mask, W, axis=0)
    offdiag = -(product.T * wide_mask)
    blocks = product.reshape(NA, S, W)
    total = jnp.einsum("nsv,nsw->svw", blocks, lhat.astype(jnp.float32), precision=lax.Precision.HIGHEST)
    diag = pivot_inverse + total
    return offdiag, diag
```

```python
import functools

import jax
import jax.numpy as jnp
from jax import lax
from jax.experimental import pallas as pl
from jax.experimental.pallas import tpu as pltpu
from jax.sharding import PartitionSpec as P

BLOCK = 128
AXES = ("prow", "pcol")
VMEM = pltpu.VMEM
SMEM = pltpu.SMEM


def whole(space):
    return pl.BlockSpec(memory_space=space)


def normalize_kernel(n, listed, panel, unit, *outs):
    p = lax.axis_index("prow")
    c = lax.axis_index("pcol")
    part = panel.shape[0] // n
    per = part // BLOCK
    for a in range(n):
        g = p ^ a
        rows = panel[pl.ds(pl.multiple_of(g * part, part), part), :]
        t = lax.dot_general(unit[0], rows, (((0,), (1,)), ((), ())), preferred_element_type=jnp.float32)
        for b in range(per):
            keep = listed[c, (p * n + g) * per + b].astype(jnp.float32)
            v = (t[:, b * BLOCK : (b + 1) * BLOCK] * keep).astype(jnp.bfloat16)
            outs[a][:, b * BLOCK : (b + 1) * BLOCK] = v
            outs[n][:, pl.ds(pl.multiple_of(g * part + b * BLOCK, BLOCK), BLOCK)] = v


def normalize(n, listed, panel, unit):
    rows, width = panel.shape
    part = rows // n
    shapes = [jax.ShapeDtypeStruct((width, part), jnp.bfloat16)] * n + [jax.ShapeDtypeStruct((width, rows), jnp.bfloat16)]
    return pl.pallas_call(
        functools.partial(normalize_kernel, n),
        out_shape=shapes,
        in_specs=[whole(SMEM), whole(VMEM), whole(VMEM)],
        out_specs=[whole(VMEM)] * (n + 1),
        cost_estimate=pl.CostEstimate(flops=2 * rows * width * width, bytes_accessed=6 * rows * width, transcendentals=0),
        name="normalize",
    )(listed, panel, unit)


def pick_kernel(n, q, *refs):
    ins, outs, held = refs[:n], refs[n : 2 * n], refs[2 * n]
    p = lax.axis_index("prow")
    z = lax.axis_index("pcol") // q
    for a in range(n):
        held[a] = ins[a][...]
    for m in range(n):
        outs[m][...] = held[p ^ z ^ m]


def pick(n, q, pieces):
    shape = pieces[0].shape
    return pl.pallas_call(
        functools.partial(pick_kernel, n, q),
        out_shape=[jax.ShapeDtypeStruct(shape, jnp.bfloat16)] * n,
        in_specs=[whole(VMEM)] * n,
        out_specs=[whole(VMEM)] * n,
        scratch_shapes=[pltpu.VMEM((n,) + shape, jnp.bfloat16)],
        cost_estimate=pl.CostEstimate(flops=0, bytes_accessed=4 * n * shape[0] * shape[1], transcendentals=0),
        name="pick",
    )(*pieces)


def partial_kernel(n, q, *refs):
    ins, tiles, out, held = refs[:n], refs[n : n + q], refs[n + q], refs[n + q + 1]
    p = lax.axis_index("prow")
    core = lax.axis_index("pcol") % q
    part = ins[0].shape[1]

    @pl.when(pl.program_id(0) == 0)
    def _():
        for a in range(n):
            held[a] = ins[a][...]

    total = None
    for e in range(q):
        for h in range(n // q):
            g = (core ^ e) * (n // q) + h
            term = lax.dot_general(
                held[g ^ p],
                tiles[e][:, h * part : (h + 1) * part],
                (((1,), (1,)), ((), ())),
                preferred_element_type=jnp.float32,
            )
            total = term if total is None else total + term
    out[...] = total.astype(out.dtype)


def partial_product(n, q, pieces, tiles, dtype):
    width, part = pieces[0].shape
    rows, depth = tiles[0].shape
    step = min(rows, 512)
    fixed = pl.BlockSpec((width, part), lambda i: (0, 0))
    return pl.pallas_call(
        functools.partial(partial_kernel, n, q),
        grid=(rows // step,),
        out_shape=jax.ShapeDtypeStruct((width, rows), dtype),
        in_specs=[fixed] * n + [pl.BlockSpec((step, depth), lambda i: (i, 0))] * q,
        out_specs=pl.BlockSpec((width, step), lambda i: (0, i)),
        scratch_shapes=[pltpu.VMEM((n, width, part), jnp.bfloat16)],
        cost_estimate=pl.CostEstimate(
            flops=2 * rows * width * depth * q, bytes_accessed=2 * q * rows * depth, transcendentals=0
        ),
        name="partial_product",
    )(*pieces, *tiles)


def finish_kernel(count, listed, lhat, *refs):
    parts, off, diag = refs[:count], refs[count], refs[count + 1]
    p = lax.axis_index("prow")
    c = lax.axis_index("pcol")
    i = pl.program_id(0)
    step = off.shape[1]
    per = step // BLOCK
    x = parts[0][...].astype(jnp.float32)
    for r in parts[1:]:
        x = x + r[...].astype(jnp.float32)
    base = (p * pl.num_programs(0) + i) * per
    for b in range(per):
        keep = listed[c, base + b].astype(jnp.float32)
        off[:, b * BLOCK : (b + 1) * BLOCK] = -(x[:, b * BLOCK : (b + 1) * BLOCK] * keep)
    high = x.astype(jnp.bfloat16)
    low = (x - high.astype(jnp.float32)).astype(jnp.bfloat16)
    dims = (((1,), (1,)), ((), ()))
    term = lax.dot_general(high, lhat[...], dims, preferred_element_type=jnp.float32)
    term = term + lax.dot_general(low, lhat[...], dims, preferred_element_type=jnp.float32)

    @pl.when(i == 0)
    def _():
        diag[...] = term

    @pl.when(i > 0)
    def _():
        diag[...] += term


def finish(listed, lhat, parts):
    width, rows = lhat.shape
    step = min(rows, 512)
    block = pl.BlockSpec((width, step), lambda i: (0, i))
    return pl.pallas_call(
        functools.partial(finish_kernel, len(parts)),
        grid=(rows // step,),
        out_shape=[
            jax.ShapeDtypeStruct((width, rows), jnp.float32),
            jax.ShapeDtypeStruct((width, width), jnp.float32),
        ],
        in_specs=[whole(SMEM)] + [block] * (1 + len(parts)),
        out_specs=[block, pl.BlockSpec((width, width), lambda i: (0, 0))],
        cost_estimate=pl.CostEstimate(flops=4 * rows * width * width, bytes_accessed=14 * rows * width, transcendentals=0),
        name="finish",
    )(listed, lhat, *parts)


def per_device(n, ncol, l_panel, inverse_tile, unit_inverse, pivot_inverse, listed):
    q = ncol // n
    devices = [(p, z, k) for p in range(n) for z in range(n) for k in range(q)]

    def at(p, z, k):
        return p * ncol + z * q + k

    def swap(x, move):
        pairs = []
        for d in devices:
            to = move(*d)
            if to is not None:
                pairs.append((at(*d), at(*to)))
        return lax.ppermute(x, AXES, pairs)

    def over_rows(x, a):
        return swap(x, lambda p, z, k: (p ^ a, z, k))

    tiles = [inverse_tile] + [swap(inverse_tile, lambda p, z, k: (p, z, k ^ e)) for e in range(1, q)]

    *pieces, lhat = normalize(n, listed, l_panel, unit_inverse)
    scattered = [pieces[0]] + [over_rows(pieces[a], a) for a in range(1, n)]
    chosen = pick(n, q, scattered)
    chunk = [None] * n
    for m in reversed(range(n)):
        mine = chosen[m] if m == 0 else swap(chosen[m], lambda p, z, k: (p, z ^ m, k))
        quarters = [mine] + [over_rows(mine, a) for a in range(1, n)]
        chunk[m] = partial_product(n, q, quarters, tiles, jnp.float32 if m == 0 else jnp.bfloat16)

    z_here = lax.axis_index("pcol") // q

    def own(odd, d):
        at_mask = {}
        for z in range(n):
            to = z + d if (z % 2) == odd else z - d
            if 0 <= to < n:
                at_mask.setdefault(z ^ to, []).append(z)
        masks = sorted(at_mask)
        x = chunk[masks[0]]
        for m in masks[1:]:
            here = functools.reduce(jnp.logical_or, [z_here == z for z in at_mask[m]])
            x = jnp.where(here, chunk[m], x)
        return x

    def add(x, y):
        if y is None:
            return x
        return (x.astype(jnp.float32) + y.astype(jnp.float32)).astype(jnp.bfloat16)

    came = [None, None]
    for d in range(n - 1, 0, -1):
        sent = [None, None]
        for odd in (0, 1):
            pairs = [z for z in range(odd, n - 1, 2) if z + d < n or z + 1 - d >= 0]
            if not pairs:
                continue
            to = {}
            for z in pairs:
                to[z], to[z + 1] = z + 1, z
            load = add(own(odd, d), came[1 - odd])
            sent[odd] = swap(load, lambda p, z, k: (p, to[z], k) if z in to else None)
        came = sent

    off, part = finish(listed, lhat, [chunk[0]] + [x for x in came if x is not None])
    travel = part.astype(jnp.bfloat16)
    total = part
    for a in range(1, n):
        total = total + over_rows(travel, a).astype(jnp.float32)
    return off, pivot_inverse + total[None]


def solution(mesh):
    n, ncol = mesh.shape["prow"], mesh.shape["pcol"]
    return jax.shard_map(
        functools.partial(per_device, n, ncol),
        mesh=mesh,
        in_specs=(
            P("prow", "pcol"),
            P("prow", "pcol"),
            P("pcol", None, None),
            P("pcol", None, None),
            P(),
        ),
        out_specs=(P("pcol", "prow"), P("pcol", None, None)),
        check_vma=False,
    )
```

```python
import functools

import jax
import jax.numpy as jnp
from jax import lax
from jax.experimental import pallas as pl
from jax.experimental.pallas import tpu as pltpu
from jax.sharding import PartitionSpec as P


BLOCK = 128
AXES = ("prow", "pcol")
VMEM = pltpu.VMEM
SMEM = pltpu.SMEM
LIMIT = 24 << 20


def whole(space):
    return pl.BlockSpec(memory_space=space)


def normalize_kernel(n, listed, panel, unit, *refs):
    outs, rows, right, keeps, came = refs[: n + 1], refs[n + 1], refs[n + 2], refs[n + 3], refs[n + 4]
    p = lax.axis_index("prow")
    c = lax.axis_index("pcol")
    part = panel.shape[0] // n
    per = part // BLOCK
    order = list(range(1, n)) + [0]
    first = [
        pltpu.make_async_copy(unit.at[0], right, came.at[n]),
        pltpu.make_async_copy(listed.at[pl.ds(c, 1), :], keeps, came.at[n + 1]),
    ]
    take = [
        pltpu.make_async_copy(panel.at[pl.ds(pl.multiple_of((p ^ a) * part, part), part), :], rows.at[a], came.at[a])
        for a in order
    ]
    for x in first + take:
        x.start()
    for x in first:
        x.wait()
    for a, x in zip(order, take):
        x.wait()
        g = p ^ a
        t = jnp.dot(rows[a], right[...], preferred_element_type=jnp.float32)
        for b in range(per):
            keep = keeps[0, (p * n + g) * per + b].astype(jnp.float32)
            v = (t[b * BLOCK : (b + 1) * BLOCK] * keep).astype(jnp.bfloat16)
            outs[a][b * BLOCK : (b + 1) * BLOCK, :] = v
            outs[n][pl.ds(pl.multiple_of(g * part + b * BLOCK, BLOCK), BLOCK), :] = v


def normalize(n, listed, panel, unit):
    rows, width = panel.shape
    part = rows // n
    shapes = [jax.ShapeDtypeStruct((part, width), jnp.bfloat16)] * n + [jax.ShapeDtypeStruct((rows, width), jnp.bfloat16)]
    return pl.pallas_call(
        functools.partial(normalize_kernel, n),
        out_shape=shapes,
        in_specs=[whole(pltpu.HBM)] * 3,
        out_specs=[whole(VMEM)] * (n + 1),
        scratch_shapes=[
            pltpu.VMEM((n, part, width), jnp.bfloat16),
            pltpu.VMEM((width, width), jnp.bfloat16),
            pltpu.SMEM((1, listed.shape[1]), jnp.int32),
            pltpu.SemaphoreType.DMA((n + 2,)),
        ],
        compiler_params=pltpu.CompilerParams(vmem_limit_bytes=LIMIT),
        cost_estimate=pl.CostEstimate(flops=2 * rows * width * width, bytes_accessed=6 * rows * width, transcendentals=0),
        name="normalize",
    )(listed, panel, unit)


def load_kernel(tile, out, came):
    x = pltpu.make_async_copy(tile, out, came)
    x.start()
    x.wait()


def load(tile):
    return pl.pallas_call(
        load_kernel,
        out_shape=jax.ShapeDtypeStruct(tile.shape, tile.dtype),
        in_specs=[whole(pltpu.HBM)],
        out_specs=whole(VMEM),
        scratch_shapes=[pltpu.SemaphoreType.DMA],
        compiler_params=pltpu.CompilerParams(vmem_limit_bytes=LIMIT),
        cost_estimate=pl.CostEstimate(flops=0, bytes_accessed=4 * tile.shape[0] * tile.shape[1], transcendentals=0),
        name="load",
    )(tile)


def pick_kernel(n, q, *refs):
    ins, outs, held, came, left = refs[:n], refs[n : 2 * n], refs[2 * n], refs[2 * n + 1], refs[2 * n + 2]
    p = lax.axis_index("prow")
    z = lax.axis_index("pcol") // q
    take = [pltpu.make_async_copy(ins[a], held.at[a], came.at[a]) for a in range(n)]
    for x in take:
        x.start()
    for x in take:
        x.wait()
    give = [pltpu.make_async_copy(held.at[p ^ z ^ m], outs[m], left.at[m]) for m in reversed(range(n))]
    for x in give:
        x.start()
    for x in give:
        x.wait()


def pick(n, q, pieces):
    shape = pieces[0].shape
    return pl.pallas_call(
        functools.partial(pick_kernel, n, q),
        out_shape=[jax.ShapeDtypeStruct(shape, jnp.bfloat16)] * n,
        in_specs=[whole(pl.ANY)] * n,
        out_specs=[whole(pl.ANY)] * n,
        scratch_shapes=[
            pltpu.VMEM((n,) + shape, jnp.bfloat16),
            pltpu.SemaphoreType.DMA((n,)),
            pltpu.SemaphoreType.DMA((n,)),
        ],
        cost_estimate=pl.CostEstimate(flops=0, bytes_accessed=4 * n * shape[0] * shape[1], transcendentals=0),
        compiler_params=pltpu.CompilerParams(vmem_limit_bytes=LIMIT),
        name="pick",
    )(*pieces)


def partial_kernel(n, q, step, *refs):
    ins, tiles, out, held, came = refs[:n], refs[n : n + q], refs[n + q], refs[n + q + 1], refs[n + q + 2]
    p = lax.axis_index("prow")
    core = lax.axis_index("pcol") % q
    part = ins[0].shape[0]
    take = [
        pltpu.make_async_copy(ins[a], held.at[pl.ds(pl.multiple_of((a ^ p) * part, part), part), :], came.at[a])
        for a in range(n)
    ]
    for x in take:
        x.start()
    for x in take:
        x.wait()
    rows, depth = tiles[0].shape
    for i in range(rows // step):
        total = None
        for e in range(q):
            right = held[pl.ds(pl.multiple_of((core ^ e) * depth, depth), depth), :]
            term = jnp.dot(tiles[e][i * step : (i + 1) * step, :], right, preferred_element_type=jnp.float32)
            total = term if total is None else total + term
        out[i * step : (i + 1) * step, :] = total.astype(out.dtype)


def partial_product(n, q, pieces, tiles, dtype):
    part, width = pieces[0].shape
    rows, depth = tiles[0].shape
    return pl.pallas_call(
        functools.partial(partial_kernel, n, q, min(rows, 512)),
        out_shape=jax.ShapeDtypeStruct((rows, width), dtype),
        in_specs=[whole(pl.ANY)] * n + [whole(VMEM)] * q,
        out_specs=whole(VMEM),
        scratch_shapes=[pltpu.VMEM((n * part, width), jnp.bfloat16), pltpu.SemaphoreType.DMA((n,))],
        compiler_params=pltpu.CompilerParams(vmem_limit_bytes=LIMIT),
        cost_estimate=pl.CostEstimate(
            flops=2 * rows * width * depth * q, bytes_accessed=2 * q * rows * depth, transcendentals=0
        ),
        name="partial_product",
    )(*pieces, *tiles)


def diagonal_kernel(count, lhat, *refs):
    parts, product, diag, sent = refs[:count], refs[count], refs[count + 1], refs[count + 2]
    rows, _ = lhat.shape
    step = min(rows, 512)
    total = None
    for i in range(rows // step):
        here = slice(i * step, (i + 1) * step)
        x = parts[0][here, :].astype(jnp.float32)
        for r in parts[1:]:
            x = x + r[here, :].astype(jnp.float32)
        x = x.T
        product[:, here] = x
        high = x.astype(jnp.bfloat16)
        low = (x - high.astype(jnp.float32)).astype(jnp.bfloat16)
        for y in (high, low):
            term = jnp.dot(y, lhat[here, :], preferred_element_type=jnp.float32)
            total = term if total is None else total + term
    diag[...] = total
    sent[...] = total.astype(jnp.bfloat16)


def diagonal(lhat, parts):
    rows, width = lhat.shape
    return pl.pallas_call(
        functools.partial(diagonal_kernel, len(parts)),
        out_shape=[
            jax.ShapeDtypeStruct((width, rows), jnp.float32),
            jax.ShapeDtypeStruct((width, width), jnp.float32),
            jax.ShapeDtypeStruct((width, width), jnp.bfloat16),
        ],
        in_specs=[whole(VMEM)] * (1 + len(parts)),
        out_specs=[whole(VMEM)] * 3,
        compiler_params=pltpu.CompilerParams(vmem_limit_bytes=LIMIT),
        cost_estimate=pl.CostEstimate(flops=4 * rows * width * width, bytes_accessed=10 * rows * width, transcendentals=0),
        name="diagonal",
    )(lhat, *parts)


def masked_kernel(listed, product, off):
    p = lax.axis_index("prow")
    c = lax.axis_index("pcol")
    i = pl.program_id(0)
    per = off.shape[1] // BLOCK
    base = (p * pl.num_programs(0) + i) * per
    for b in range(per):
        keep = listed[c, base + b].astype(jnp.float32)
        off[:, b * BLOCK : (b + 1) * BLOCK] = -(product[:, b * BLOCK : (b + 1) * BLOCK] * keep)


def masked(listed, product):
    width, rows = product.shape
    step = min(rows, 1024)
    block = pl.BlockSpec((width, step), lambda i: (0, i))
    return pl.pallas_call(
        masked_kernel,
        grid=(rows // step,),
        out_shape=jax.ShapeDtypeStruct((width, rows), jnp.float32),
        in_specs=[whole(SMEM), block],
        out_specs=block,
        compiler_params=pltpu.CompilerParams(vmem_limit_bytes=LIMIT),
        cost_estimate=pl.CostEstimate(flops=2 * rows * width, bytes_accessed=8 * rows * width, transcendentals=0),
        name="masked",
    )(listed, product)


def per_device(n, ncol, l_panel, inverse_tile, unit_inverse, pivot_inverse, listed):
    return level(n, ncol, l_panel, inverse_tile, unit_inverse, pivot_inverse, listed)


def level(n, ncol, l_panel, inverse_tile, unit_inverse, pivot_inverse, listed):
    q = ncol // n
    devices = [(p, z, k) for p in range(n) for z in range(n) for k in range(q)]

    def at(p, z, k):
        return p * ncol + z * q + k

    def swap(x, move):
        pairs = []
        for d in devices:
            to = move(*d)
            if to is not None:
                pairs.append((at(*d), at(*to)))
        return lax.ppermute(x, AXES, pairs)

    def over_rows(x, a):
        return swap(x, lambda p, z, k: (p ^ a, z, k))

    *pieces, lhat = normalize(n, listed, l_panel, unit_inverse)
    tiles = [load(inverse_tile)]
    tiles += [swap(inverse_tile, lambda p, z, k: (p, z, k ^ e)) for e in range(1, q)]
    tiles = [pltpu.with_memory_space_constraint(t, pltpu.VMEM) for t in tiles]

    scattered = [pieces[0]] + [over_rows(pieces[a], a) for a in range(1, n)]
    chosen = pick(n, q, scattered)
    chunk = [None] * n
    for m in reversed(range(n)):
        mine = chosen[m] if m == 0 else swap(chosen[m], lambda p, z, k: (p, z ^ m, k))
        quarters = [mine] + [over_rows(mine, a) for a in range(1, n)]
        chunk[m] = partial_product(n, q, quarters, tiles, jnp.float32 if m == 0 else jnp.bfloat16)

    z_here = lax.axis_index("pcol") // q

    def own(odd, d):
        at_mask = {}
        for z in range(n):
            to = z + d if (z % 2) == odd else z - d
            if 0 <= to < n:
                at_mask.setdefault(z ^ to, []).append(z)
        masks = sorted(at_mask)
        x = chunk[masks[0]]
        for m in masks[1:]:
            here = functools.reduce(jnp.logical_or, [z_here == z for z in at_mask[m]])
            x = jnp.where(here, chunk[m], x)
        return x

    def add(x, y):
        if y is None:
            return x
        return (x.astype(jnp.float32) + y.astype(jnp.float32)).astype(jnp.bfloat16)

    came = [None, None]
    for d in range(n - 1, 0, -1):
        sent = [None, None]
        for odd in (0, 1):
            pairs = line_pairs(n, d, odd)
            if not pairs:
                continue
            to = {}
            for z in pairs:
                to[z], to[z + 1] = z + 1, z
            load_ = add(own(odd, d), came[1 - odd])
            sent[odd] = swap(load_, lambda p, z, k: (p, to[z], k) if z in to else None)
        came = sent

    product, part, travel = diagonal(lhat, [chunk[0]] + [x for x in came if x is not None])
    off = masked(listed, product)
    total = part
    for a in range(1, n):
        total = total + over_rows(travel, a).astype(jnp.float32)
    return off, pivot_inverse + total[None]


def line_pairs(n, d, odd):
    return [z for z in range(odd, n - 1, 2) if z + d < n or z + 1 - d >= 0]


def solution(mesh):
    n, ncol = mesh.shape["prow"], mesh.shape["pcol"]
    return jax.shard_map(
        functools.partial(per_device, n, ncol),
        mesh=mesh,
        in_specs=(
            P("prow", "pcol"),
            P("prow", "pcol"),
            P("pcol", None, None),
            P("pcol", None, None),
            P(),
        ),
        out_specs=(P("pcol", "prow"), P("pcol", None, None)),
        check_vma=False,
    )
```

```python
import functools

import jax
import jax.numpy as jnp
from jax import lax
from jax.experimental import pallas as pl
from jax.experimental.pallas import tpu as pltpu
from jax.sharding import PartitionSpec as P


BLOCK = 128
AXES = ("prow", "pcol")
VMEM = pltpu.VMEM
SMEM = pltpu.SMEM
LIMIT = 24 << 20
HALVES = 2


def whole(space):
    return pl.BlockSpec(memory_space=space)


def normalize_kernel(n, listed, panel, unit, *refs):
    outs, rows, right, keeps, came = refs[: n + 1], refs[n + 1], refs[n + 2], refs[n + 3], refs[n + 4]
    p = lax.axis_index("prow")
    c = lax.axis_index("pcol")
    part = panel.shape[0] // n
    per = part // BLOCK
    order = list(range(1, n)) + [0]
    first = [
        pltpu.make_async_copy(unit.at[0], right, came.at[n]),
        pltpu.make_async_copy(listed.at[pl.ds(c, 1), :], keeps, came.at[n + 1]),
    ]
    take = [
        pltpu.make_async_copy(panel.at[pl.ds(pl.multiple_of((p ^ a) * part, part), part), :], rows.at[a], came.at[a])
        for a in order
    ]
    for x in first + take:
        x.start()
    for x in first:
        x.wait()
    for a, x in zip(order, take):
        x.wait()
        g = p ^ a
        t = jnp.dot(rows[a], right[...], preferred_element_type=jnp.float32)
        for b in range(per):
            keep = keeps[0, (p * n + g) * per + b].astype(jnp.float32)
            v = (t[b * BLOCK : (b + 1) * BLOCK] * keep).astype(jnp.bfloat16)
            outs[a][b * BLOCK : (b + 1) * BLOCK, :] = v
            outs[n][pl.ds(pl.multiple_of(g * part + b * BLOCK, BLOCK), BLOCK), :] = v


def normalize(n, listed, panel, unit):
    rows, width = panel.shape
    part = rows // n
    shapes = [jax.ShapeDtypeStruct((part, width), jnp.bfloat16)] * n + [jax.ShapeDtypeStruct((rows, width), jnp.bfloat16)]
    return pl.pallas_call(
        functools.partial(normalize_kernel, n),
        out_shape=shapes,
        in_specs=[whole(pltpu.HBM)] * 3,
        out_specs=[whole(VMEM)] * (n + 1),
        scratch_shapes=[
            pltpu.VMEM((n, part, width), jnp.bfloat16),
            pltpu.VMEM((width, width), jnp.bfloat16),
            pltpu.SMEM((1, listed.shape[1]), jnp.int32),
            pltpu.SemaphoreType.DMA((n + 2,)),
        ],
        compiler_params=pltpu.CompilerParams(vmem_limit_bytes=LIMIT),
        cost_estimate=pl.CostEstimate(flops=2 * rows * width * width, bytes_accessed=6 * rows * width, transcendentals=0),
        name="normalize",
    )(listed, panel, unit)


def load_kernel(tile, out, came):
    x = pltpu.make_async_copy(tile, out, came)
    x.start()
    x.wait()


def load(tile):
    return pl.pallas_call(
        load_kernel,
        out_shape=jax.ShapeDtypeStruct(tile.shape, tile.dtype),
        in_specs=[whole(pltpu.HBM)],
        out_specs=whole(VMEM),
        scratch_shapes=[pltpu.SemaphoreType.DMA],
        compiler_params=pltpu.CompilerParams(vmem_limit_bytes=LIMIT),
        cost_estimate=pl.CostEstimate(flops=0, bytes_accessed=4 * tile.shape[0] * tile.shape[1], transcendentals=0),
        name="load",
    )(tile)


def pick_kernel(n, q, *refs):
    ins, outs, held, came, left = refs[:n], refs[n : 2 * n], refs[2 * n], refs[2 * n + 1], refs[2 * n + 2]
    p = lax.axis_index("prow")
    z = lax.axis_index("pcol") // q
    take = [pltpu.make_async_copy(ins[a], held.at[a], came.at[a]) for a in range(n)]
    for x in take:
        x.start()
    for x in take:
        x.wait()
    give = [pltpu.make_async_copy(held.at[p ^ z ^ m], outs[m], left.at[m]) for m in reversed(range(n))]
    for x in give:
        x.start()
    for x in give:
        x.wait()


def pick(n, q, pieces):
    shape = pieces[0].shape
    return pl.pallas_call(
        functools.partial(pick_kernel, n, q),
        out_shape=[jax.ShapeDtypeStruct(shape, jnp.bfloat16)] * n,
        in_specs=[whole(pl.ANY)] * n,
        out_specs=[whole(pl.ANY)] * n,
        scratch_shapes=[
            pltpu.VMEM((n,) + shape, jnp.bfloat16),
            pltpu.SemaphoreType.DMA((n,)),
            pltpu.SemaphoreType.DMA((n,)),
        ],
        compiler_params=pltpu.CompilerParams(vmem_limit_bytes=LIMIT),
        cost_estimate=pl.CostEstimate(flops=0, bytes_accessed=4 * n * shape[0] * shape[1], transcendentals=0),
        name="pick",
    )(*pieces)


def partial_kernel(n, q, halves, step, *refs):
    ins, tiles = refs[:n], refs[n : n + q]
    outs, held, came = refs[n + q : -2], refs[-2], refs[-1]
    p = lax.axis_index("prow")
    core = lax.axis_index("pcol") % q
    chunks, part, width = ins[0].shape
    take = [
        pltpu.make_async_copy(
            ins[a].at[k],
            held.at[pl.ds(pl.multiple_of((a ^ p) * part, part), part), k * width : (k + 1) * width],
            came.at[a * chunks + k],
        )
        for a in range(n)
        for k in range(chunks)
    ]
    for x in take:
        x.start()
    for x in take:
        x.wait()
    rows, depth = tiles[0].shape
    tall = rows // HALVES
    for i, h in enumerate(halves):
        for r in range(tall // step):
            base = h * tall + r * step
            total = None
            for e in range(q):
                right = held[pl.ds(pl.multiple_of((core ^ e) * depth, depth), depth), :]
                term = jnp.dot(tiles[e][base : base + step, :], right, preferred_element_type=jnp.float32)
                total = term if total is None else total + term
            for k in range(chunks):
                outs[k * len(halves) + i][r * step : (r + 1) * step, :] = total[:, k * width : (k + 1) * width].astype(
                    jnp.bfloat16
                )


def partial_product(n, q, halves, pieces, tiles):
    chunks, part, width = pieces[0].shape
    rows, depth = tiles[0].shape
    tall = rows // HALVES
    outs = pl.pallas_call(
        functools.partial(partial_kernel, n, q, halves, min(tall, 512)),
        out_shape=[jax.ShapeDtypeStruct((tall, width), jnp.bfloat16)] * (chunks * len(halves)),
        in_specs=[whole(pl.ANY)] * n + [whole(VMEM)] * q,
        out_specs=[whole(VMEM)] * (chunks * len(halves)),
        scratch_shapes=[
            pltpu.VMEM((n * part, chunks * width), jnp.bfloat16),
            pltpu.SemaphoreType.DMA((n * chunks,)),
        ],
        compiler_params=pltpu.CompilerParams(vmem_limit_bytes=LIMIT),
        cost_estimate=pl.CostEstimate(
            flops=2 * tall * len(halves) * width * chunks * depth * q,
            bytes_accessed=2 * q * tall * len(halves) * depth,
            transcendentals=0,
        ),
        name="partial_product",
    )(*pieces, *tiles)
    return [list(outs[k * len(halves) : (k + 1) * len(halves)]) for k in range(chunks)]


def diagonal_kernel(lhat, *refs):
    ins, product, diag, sent = refs[:-3], refs[-3], refs[-2], refs[-1]
    count = len(ins) // HALVES
    tall = ins[0].shape[0]
    step = min(tall, 512)
    total = None
    for h in range(HALVES):
        first, *came = ins[h * count : (h + 1) * count]
        for r in range(tall // step):
            here = slice(r * step, (r + 1) * step)
            there = slice(h * tall + r * step, h * tall + (r + 1) * step)
            x = first[here, :].astype(jnp.float32)
            for y in came:
                x = x + y[here, :].astype(jnp.float32)
            x = x.T
            product[:, there] = x
            high = x.astype(jnp.bfloat16)
            low = (x - high.astype(jnp.float32)).astype(jnp.bfloat16)
            for y in (high, low):
                term = jnp.dot(y, lhat[there, :], preferred_element_type=jnp.float32)
                total = term if total is None else total + term
    diag[...] = total
    sent[...] = total.astype(jnp.bfloat16)


def diagonal(lhat, parts):
    rows, width = lhat.shape
    ins = [x for half in parts for x in half]
    return pl.pallas_call(
        diagonal_kernel,
        out_shape=[
            jax.ShapeDtypeStruct((width, rows), jnp.float32),
            jax.ShapeDtypeStruct((width, width), jnp.float32),
            jax.ShapeDtypeStruct((width, width), jnp.bfloat16),
        ],
        in_specs=[whole(VMEM)] * (1 + len(ins)),
        out_specs=[whole(VMEM)] * 3,
        compiler_params=pltpu.CompilerParams(vmem_limit_bytes=LIMIT),
        cost_estimate=pl.CostEstimate(flops=4 * rows * width * width, bytes_accessed=10 * rows * width, transcendentals=0),
        name="diagonal",
    )(lhat, *ins)


def masked_kernel(listed, product, off):
    p = lax.axis_index("prow")
    c = lax.axis_index("pcol")
    i = pl.program_id(0)
    per = off.shape[1] // BLOCK
    base = (p * pl.num_programs(0) + i) * per
    for b in range(per):
        keep = listed[c, base + b].astype(jnp.float32)
        off[:, b * BLOCK : (b + 1) * BLOCK] = -(product[:, b * BLOCK : (b + 1) * BLOCK] * keep)


def masked(listed, product):
    width, rows = product.shape
    step = min(rows, 1024)
    block = pl.BlockSpec((width, step), lambda i: (0, i))
    return pl.pallas_call(
        masked_kernel,
        grid=(rows // step,),
        out_shape=jax.ShapeDtypeStruct((width, rows), jnp.float32),
        in_specs=[whole(SMEM), block],
        out_specs=block,
        compiler_params=pltpu.CompilerParams(vmem_limit_bytes=LIMIT),
        cost_estimate=pl.CostEstimate(flops=2 * rows * width, bytes_accessed=8 * rows * width, transcendentals=0),
        name="masked",
    )(listed, product)


def per_device(n, ncol, l_panel, inverse_tile, unit_inverse, pivot_inverse, listed):
    return level(n, ncol, l_panel, inverse_tile, unit_inverse, pivot_inverse, listed)


def level(n, ncol, l_panel, inverse_tile, unit_inverse, pivot_inverse, listed):
    q = ncol // n
    devices = [(p, z, k) for p in range(n) for z in range(n) for k in range(q)]

    def at(p, z, k):
        return p * ncol + z * q + k

    def swap(x, move):
        pairs = []
        for d in devices:
            to = move(*d)
            if to is not None:
                pairs.append((at(*d), at(*to)))
        return lax.ppermute(x, AXES, pairs)

    def over_rows(x, a):
        return swap(x, lambda p, z, k: (p ^ a, z, k))

    *pieces, lhat = normalize(n, listed, l_panel, unit_inverse)
    tiles = [load(inverse_tile)]
    tiles += [swap(inverse_tile, lambda p, z, k: (p, z, k ^ e)) for e in range(1, q)]
    tiles = [pltpu.with_memory_space_constraint(t, pltpu.VMEM) for t in tiles]

    scattered = [pieces[0]] + [over_rows(pieces[a], a) for a in range(1, n)]
    chosen = pick(n, q, scattered)

    mine = [chosen[0]] + [swap(chosen[m], lambda p, z, k: (p, z ^ m, k)) for m in range(1, n)]
    chunk = [None] * n
    for i, group in enumerate(groups(n)):
        load_ = jnp.stack([mine[m] for m in group])
        quarters = [load_] + [over_rows(load_, a) for a in range(1, n)]
        if i == 1:
            chunk[group[0]] = []
            for h in range(HALVES):
                chunk[group[0]] += partial_product(n, q, (h,), quarters, tiles)[0]
        else:
            done = partial_product(n, q, tuple(range(HALVES)), quarters, tiles)
            for m, x in zip(group, done):
                chunk[m] = x

    z_here = lax.axis_index("pcol") // q

    def own(odd, d, h):
        at_mask = {}
        for z in range(n):
            to = z + d if (z % 2) == odd else z - d
            if 0 <= to < n:
                at_mask.setdefault(z ^ to, []).append(z)
        masks = sorted(at_mask)
        x = chunk[masks[0]][h]
        for m in masks[1:]:
            here = functools.reduce(jnp.logical_or, [z_here == z for z in at_mask[m]])
            x = jnp.where(here, chunk[m][h], x)
        return x

    def add(x, y):
        if y is None:
            return x
        return (x.astype(jnp.float32) + y.astype(jnp.float32)).astype(jnp.bfloat16)

    came = [[None, None] for _ in range(HALVES)]
    for d in range(n - 1, 0, -1):
        for h in range(HALVES):
            sent = [None, None]
            for odd in (0, 1):
                pairs = line_pairs(n, d, odd)
                if not pairs:
                    continue
                to = {}
                for z in pairs:
                    to[z], to[z + 1] = z + 1, z
                load_ = add(own(odd, d, h), came[h][1 - odd])
                sent[odd] = swap(load_, lambda p, z, k: (p, to[z], k) if z in to else None)
            came[h] = sent

    parts = [[chunk[0][h]] + [x for x in came[h] if x is not None] for h in range(HALVES)]
    product, part, travel = diagonal(lhat, parts)
    off = masked(listed, product)
    total = part
    for a in range(1, n):
        total = total + over_rows(travel, a).astype(jnp.float32)
    return off, pivot_inverse + total[None]


def groups(n):
    return [[0], [n - 1]] + [[m for m in (b, b - 1) if m > 0] for b in range(n - 2, 0, -2)]


def line_pairs(n, d, odd):
    return [z for z in range(odd, n - 1, 2) if z + d < n or z + 1 - d >= 0]


def solution(mesh):
    n, ncol = mesh.shape["prow"], mesh.shape["pcol"]
    return jax.shard_map(
        functools.partial(per_device, n, ncol),
        mesh=mesh,
        in_specs=(
            P("prow", "pcol"),
            P("prow", "pcol"),
            P("pcol", None, None),
            P("pcol", None, None),
            P(),
        ),
        out_specs=(P("pcol", "prow"), P("pcol", None, None)),
        check_vma=False,
    )
```

```python
import functools

import jax
import jax.numpy as jnp
from jax import lax
from jax.experimental import pallas as pl
from jax.experimental.pallas import tpu as pltpu
from jax.sharding import PartitionSpec as P


BLOCK = 128
AXES = ("prow", "pcol")
VMEM = pltpu.VMEM
SMEM = pltpu.SMEM
LIMIT = 24 << 20
FULL = 62 << 20
HALVES = 2


def whole(space):
    return pl.BlockSpec(memory_space=space)


def normalize_kernel(n, listed, panel, unit, *refs):
    outs, rows, right, keeps, came = refs[: n + 1], refs[n + 1], refs[n + 2], refs[n + 3], refs[n + 4]
    p = lax.axis_index("prow")
    c = lax.axis_index("pcol")
    part = panel.shape[0] // n
    per = part // BLOCK
    order = list(range(1, n)) + [0]
    first = [
        pltpu.make_async_copy(unit.at[0], right, came.at[n]),
        pltpu.make_async_copy(listed.at[pl.ds(c, 1), :], keeps, came.at[n + 1]),
    ]
    take = [
        pltpu.make_async_copy(panel.at[pl.ds(pl.multiple_of((p ^ a) * part, part), part), :], rows.at[a], came.at[a])
        for a in order
    ]
    for x in first + take:
        x.start()
    for x in first:
        x.wait()
    for a, x in zip(order, take):
        x.wait()
        g = p ^ a
        t = jnp.dot(rows[a], right[...], preferred_element_type=jnp.float32)
        for b in range(per):
            keep = keeps[0, (p * n + g) * per + b].astype(jnp.float32)
            v = (t[b * BLOCK : (b + 1) * BLOCK] * keep).astype(jnp.bfloat16)
            outs[a][b * BLOCK : (b + 1) * BLOCK, :] = v
            outs[n][pl.ds(pl.multiple_of(g * part + b * BLOCK, BLOCK), BLOCK), :] = v


def normalize(n, listed, panel, unit):
    rows, width = panel.shape
    part = rows // n
    shapes = [jax.ShapeDtypeStruct((part, width), jnp.bfloat16)] * n + [jax.ShapeDtypeStruct((rows, width), jnp.bfloat16)]
    return pl.pallas_call(
        functools.partial(normalize_kernel, n),
        out_shape=shapes,
        in_specs=[whole(pltpu.HBM)] * 3,
        out_specs=[whole(VMEM)] * (n + 1),
        scratch_shapes=[
            pltpu.VMEM((n, part, width), jnp.bfloat16),
            pltpu.VMEM((width, width), jnp.bfloat16),
            pltpu.SMEM((1, listed.shape[1]), jnp.int32),
            pltpu.SemaphoreType.DMA((n + 2,)),
        ],
        compiler_params=pltpu.CompilerParams(vmem_limit_bytes=FULL),
        cost_estimate=pl.CostEstimate(flops=2 * rows * width * width, bytes_accessed=6 * rows * width, transcendentals=0),
        name="normalize",
    )(listed, panel, unit)


def load_kernel(tile, out, came):
    x = pltpu.make_async_copy(tile, out, came)
    x.start()
    x.wait()


def load(tile):
    return pl.pallas_call(
        load_kernel,
        out_shape=jax.ShapeDtypeStruct(tile.shape, tile.dtype),
        in_specs=[whole(pltpu.HBM)],
        out_specs=whole(VMEM),
        scratch_shapes=[pltpu.SemaphoreType.DMA],
        compiler_params=pltpu.CompilerParams(vmem_limit_bytes=LIMIT),
        cost_estimate=pl.CostEstimate(flops=0, bytes_accessed=4 * tile.shape[0] * tile.shape[1], transcendentals=0),
        name="load",
    )(tile)


def pick_kernel(n, q, *refs):
    ins, outs = refs[:n], refs[n:]
    at = lax.axis_index("prow") ^ (lax.axis_index("pcol") // q)
    for b in range(n):

        @pl.when(at == b)
        def _():
            for m in range(n):
                outs[m][...] = ins[b ^ m][...]


def pick(n, q, pieces):
    shape = pieces[0].shape
    return pl.pallas_call(
        functools.partial(pick_kernel, n, q),
        out_shape=[jax.ShapeDtypeStruct(shape, jnp.bfloat16)] * n,
        in_specs=[whole(VMEM)] * n,
        out_specs=[whole(VMEM)] * n,
        compiler_params=pltpu.CompilerParams(vmem_limit_bytes=LIMIT),
        cost_estimate=pl.CostEstimate(flops=0, bytes_accessed=4 * n * shape[0] * shape[1], transcendentals=0),
        name="pick",
    )(*pieces)


def partial_kernel(n, q, halves, step, *refs):
    ins, tiles = refs[:n], refs[n : n + q]
    outs, held = refs[n + q : -1], refs[-1]
    p = lax.axis_index("prow")
    core = lax.axis_index("pcol") % q
    chunks, part, width = ins[0].shape
    for a in range(n):
        for k in range(chunks):
            held[pl.ds(pl.multiple_of((a ^ p) * part, part), part), k * width : (k + 1) * width] = ins[a][k]
    rows, depth = tiles[0].shape
    tall = rows // HALVES
    for i, h in enumerate(halves):
        for r in range(tall // step):
            base = h * tall + r * step
            total = None
            for e in range(q):
                right = held[pl.ds(pl.multiple_of((core ^ e) * depth, depth), depth), :]
                term = jnp.dot(tiles[e][base : base + step, :], right, preferred_element_type=jnp.float32)
                total = term if total is None else total + term
            for k in range(chunks):
                outs[k * len(halves) + i][r * step : (r + 1) * step, :] = total[:, k * width : (k + 1) * width].astype(
                    jnp.bfloat16
                )


def partial_product(n, q, halves, pieces, tiles):
    chunks, part, width = pieces[0].shape
    rows, depth = tiles[0].shape
    tall = rows // HALVES
    outs = pl.pallas_call(
        functools.partial(partial_kernel, n, q, halves, min(tall, 512)),
        out_shape=[jax.ShapeDtypeStruct((tall, width), jnp.bfloat16)] * (chunks * len(halves)),
        in_specs=[whole(VMEM)] * (n + q),
        out_specs=[whole(VMEM)] * (chunks * len(halves)),
        scratch_shapes=[pltpu.VMEM((n * part, chunks * width), jnp.bfloat16)],
        compiler_params=pltpu.CompilerParams(vmem_limit_bytes=LIMIT),
        cost_estimate=pl.CostEstimate(
            flops=2 * tall * len(halves) * width * chunks * depth * q,
            bytes_accessed=2 * q * tall * len(halves) * depth,
            transcendentals=0,
        ),
        name="partial_product",
    )(*pieces, *tiles)
    return [list(outs[k * len(halves) : (k + 1) * len(halves)]) for k in range(chunks)]


def piece_kernel(n, q, which, base, step, *refs):
    ins, tiles = refs[: len(which)], refs[len(which) : len(which) + q]
    before, out = refs[len(which) + q : -1], refs[-1]
    p = lax.axis_index("prow")
    core = lax.axis_index("pcol") % q
    _, part, _ = ins[0].shape
    each = n // q
    for r in range(out.shape[0] // step):
        here = slice(r * step, (r + 1) * step)
        there = slice(base + r * step, base + (r + 1) * step)
        total = before[0][there, :] if before else None
        for a, piece in zip(which, ins):
            g = a ^ p
            columns = pl.ds(pl.multiple_of((g % each) * part, part), part)
            left = tiles[0][there, columns]
            for e in range(1, q):
                left = jnp.where((core ^ e) == g // each, tiles[e][there, columns], left)
            term = jnp.dot(left, piece[0], preferred_element_type=jnp.float32)
            total = term if total is None else total + term
        out[here, :] = total.astype(out.dtype)


def piece_product(n, q, which, pieces, tiles, base, tall, before, dtype):
    _, part, width = pieces[0].shape
    return pl.pallas_call(
        functools.partial(piece_kernel, n, q, which, base, min(tall, 512)),
        out_shape=jax.ShapeDtypeStruct((tall, width), dtype),
        in_specs=[whole(VMEM)] * (len(which) + q + len(before)),
        out_specs=whole(VMEM),
        compiler_params=pltpu.CompilerParams(vmem_limit_bytes=LIMIT),
        cost_estimate=pl.CostEstimate(
            flops=2 * tall * width * part * len(which), bytes_accessed=2 * tall * part * len(which), transcendentals=0
        ),
        name="piece_product",
    )(*pieces, *tiles, *before)


def diagonal_kernel(lhat, *refs):
    ins, product, diag, sent = refs[:-3], refs[-3], refs[-2], refs[-1]
    count = len(ins) // HALVES
    tall = ins[0].shape[0]
    step = min(tall, 512)
    total = None
    for h in range(HALVES):
        first, *came = ins[h * count : (h + 1) * count]
        for r in range(tall // step):
            here = slice(r * step, (r + 1) * step)
            there = slice(h * tall + r * step, h * tall + (r + 1) * step)
            x = first[here, :].astype(jnp.float32)
            for y in came:
                x = x + y[here, :].astype(jnp.float32)
            x = x.T
            product[:, there] = x
            high = x.astype(jnp.bfloat16)
            low = (x - high.astype(jnp.float32)).astype(jnp.bfloat16)
            for y in (high, low):
                term = jnp.dot(y, lhat[there, :], preferred_element_type=jnp.float32)
                total = term if total is None else total + term
    diag[...] = total
    sent[...] = total.astype(jnp.bfloat16)


def diagonal(lhat, parts):
    rows, width = lhat.shape
    ins = [x for half in parts for x in half]
    return pl.pallas_call(
        diagonal_kernel,
        out_shape=[
            jax.ShapeDtypeStruct((width, rows), jnp.float32),
            jax.ShapeDtypeStruct((width, width), jnp.float32),
            jax.ShapeDtypeStruct((width, width), jnp.bfloat16),
        ],
        in_specs=[whole(VMEM)] * (1 + len(ins)),
        out_specs=[whole(VMEM)] * 3,
        compiler_params=pltpu.CompilerParams(vmem_limit_bytes=LIMIT),
        cost_estimate=pl.CostEstimate(flops=4 * rows * width * width, bytes_accessed=10 * rows * width, transcendentals=0),
        name="diagonal",
    )(lhat, *ins)


def masked_kernel(listed, product, off):
    p = lax.axis_index("prow")
    c = lax.axis_index("pcol")
    i = pl.program_id(0)
    per = off.shape[1] // BLOCK
    base = (p * pl.num_programs(0) + i) * per
    for b in range(per):
        keep = listed[c, base + b].astype(jnp.float32)
        off[:, b * BLOCK : (b + 1) * BLOCK] = -(product[:, b * BLOCK : (b + 1) * BLOCK] * keep)


def masked(listed, product):
    width, rows = product.shape
    step = min(rows, 1024)
    block = pl.BlockSpec((width, step), lambda i: (0, i))
    return pl.pallas_call(
        masked_kernel,
        grid=(rows // step,),
        out_shape=jax.ShapeDtypeStruct((width, rows), jnp.float32),
        in_specs=[whole(SMEM), block],
        out_specs=block,
        compiler_params=pltpu.CompilerParams(vmem_limit_bytes=LIMIT),
        cost_estimate=pl.CostEstimate(flops=2 * rows * width, bytes_accessed=8 * rows * width, transcendentals=0),
        name="masked",
    )(listed, product)


def per_device(n, ncol, l_panel, inverse_tile, unit_inverse, pivot_inverse, listed):
    return level(n, ncol, l_panel, inverse_tile, unit_inverse, pivot_inverse, listed)


def level(n, ncol, l_panel, inverse_tile, unit_inverse, pivot_inverse, listed):
    q = ncol // n
    devices = [(p, z, k) for p in range(n) for z in range(n) for k in range(q)]

    def at(p, z, k):
        return p * ncol + z * q + k

    def swap(x, move):
        pairs = []
        for d in devices:
            to = move(*d)
            if to is not None:
                pairs.append((at(*d), at(*to)))
        return lax.ppermute(x, AXES, pairs)

    def over_rows(x, a):
        return swap(x, lambda p, z, k: (p ^ a, z, k))

    *pieces, lhat = normalize(n, listed, l_panel, unit_inverse)
    tiles = [load(inverse_tile)]
    tiles += [swap(inverse_tile, lambda p, z, k: (p, z, k ^ e)) for e in range(1, q)]
    tiles = [pltpu.with_memory_space_constraint(t, pltpu.VMEM) for t in tiles]

    scattered = [pieces[0]] + [over_rows(pieces[a], a) for a in range(1, n)]
    chosen = pick(n, q, scattered)

    mine = [chosen[0]] + [swap(chosen[m], lambda p, z, k: (p, z ^ m, k)) for m in range(1, n)]
    chunk = [None] * n
    for i, group in enumerate(groups(n)):
        load_ = jnp.stack([mine[m] for m in group])
        quarters = [load_] + [over_rows(load_, a) for a in range(1, n)]
        if i == 1:
            rows = inverse_tile.shape[0]
            most = piece_product(n, q, range(n - 1), quarters[:-1], tiles, 0, rows, [], jnp.float32)
            chunk[group[0]] = []
            for h in range(HALVES):
                tall = rows // HALVES
                x = piece_product(n, q, [n - 1], quarters[-1:], tiles, h * tall, tall, [most], jnp.bfloat16)
                chunk[group[0]].append(x)
        else:
            done = partial_product(n, q, tuple(range(HALVES)), quarters, tiles)
            for m, x in zip(group, done):
                chunk[m] = x

    z_here = lax.axis_index("pcol") // q

    def own(odd, d, h):
        at_mask = {}
        for z in range(n):
            to = z + d if (z % 2) == odd else z - d
            if 0 <= to < n:
                at_mask.setdefault(z ^ to, []).append(z)
        masks = sorted(at_mask)
        x = chunk[masks[0]][h]
        for m in masks[1:]:
            here = functools.reduce(jnp.logical_or, [z_here == z for z in at_mask[m]])
            x = jnp.where(here, chunk[m][h], x)
        return x

    def add(x, y):
        if y is None:
            return x
        return (x.astype(jnp.float32) + y.astype(jnp.float32)).astype(jnp.bfloat16)

    came = [[None, None] for _ in range(HALVES)]
    for d in range(n - 1, 0, -1):
        for h in range(HALVES):
            sent = [None, None]
            for odd in (0, 1):
                pairs = line_pairs(n, d, odd)
                if not pairs:
                    continue
                to = {}
                for z in pairs:
                    to[z], to[z + 1] = z + 1, z
                load_ = add(own(odd, d, h), came[h][1 - odd])
                sent[odd] = swap(load_, lambda p, z, k: (p, to[z], k) if z in to else None)
            came[h] = sent

    parts = [[chunk[0][h]] + [x for x in came[h] if x is not None] for h in range(HALVES)]
    product, part, travel = diagonal(lhat, parts)
    off = masked(listed, product)
    total = part
    for a in range(1, n):
        total = total + over_rows(travel, a).astype(jnp.float32)
    return off, pivot_inverse + total[None]


def groups(n):
    return [[0], [n - 1]] + [[m] for m in range(n - 2, 0, -1)]


def line_pairs(n, d, odd):
    return [z for z in range(odd, n - 1, 2) if z + d < n or z + 1 - d >= 0]


def solution(mesh):
    n, ncol = mesh.shape["prow"], mesh.shape["pcol"]
    return jax.shard_map(
        functools.partial(per_device, n, ncol),
        mesh=mesh,
        in_specs=(
            P("prow", "pcol"),
            P("prow", "pcol"),
            P("pcol", None, None),
            P("pcol", None, None),
            P(),
        ),
        out_specs=(P("pcol", "prow"), P("pcol", None, None)),
        check_vma=False,
    )
```

```python
import functools

import jax
import jax.numpy as jnp
from jax import lax
from jax.experimental import pallas as pl
from jax.experimental.pallas import tpu as pltpu
from jax.sharding import PartitionSpec as P


BLOCK = 128
AXES = ("prow", "pcol")
VMEM = pltpu.VMEM
SMEM = pltpu.SMEM
LIMIT = 24 << 20
FULL = 62 << 20
HALVES = 2


def whole(space):
    return pl.BlockSpec(memory_space=space)


def normalize_kernel(n, listed, panel, unit, *refs):
    outs, (rows, right, keeps, ordered, came) = refs[:-5], refs[-5:]
    p = lax.axis_index("prow")
    c = lax.axis_index("pcol")
    part = panel.shape[0] // n
    per = part // BLOCK
    order = list(range(1, n)) + [0]
    first = [
        pltpu.make_async_copy(unit.at[0], right, came.at[n]),
        pltpu.make_async_copy(listed.at[pl.ds(c, 1), :], keeps, came.at[n + 1]),
    ]
    take = [
        pltpu.make_async_copy(panel.at[pl.ds(pl.multiple_of((p ^ a) * part, part), part), :], rows.at[a], came.at[a])
        for a in order
    ]
    for x in first + take:
        x.start()
    for x in first:
        x.wait()
    for a, x in zip(order, take):
        x.wait()
        g = p ^ a
        t = jnp.dot(rows[a], right[...], preferred_element_type=jnp.float32)
        for b in range(per):
            keep = keeps[0, (p * n + g) * per + b].astype(jnp.float32)
            v = (t[b * BLOCK : (b + 1) * BLOCK] * keep).astype(jnp.bfloat16)
            outs[a][b * BLOCK : (b + 1) * BLOCK, :] = v
            ordered[pl.ds(pl.multiple_of(g * part + b * BLOCK, BLOCK), BLOCK), :] = v
    tall = panel.shape[0] // HALVES
    for h in range(HALVES):
        outs[n + h][...] = ordered[h * tall : (h + 1) * tall, :]


def normalize(n, listed, panel, unit):
    rows, width = panel.shape
    part = rows // n
    shapes = [jax.ShapeDtypeStruct((part, width), jnp.bfloat16)] * n + [
        jax.ShapeDtypeStruct((rows // HALVES, width), jnp.bfloat16)
    ] * HALVES
    return pl.pallas_call(
        functools.partial(normalize_kernel, n),
        out_shape=shapes,
        in_specs=[whole(pltpu.HBM)] * 3,
        out_specs=[whole(VMEM)] * (n + HALVES),
        scratch_shapes=[
            pltpu.VMEM((n, part, width), jnp.bfloat16),
            pltpu.VMEM((width, width), jnp.bfloat16),
            pltpu.SMEM((1, listed.shape[1]), jnp.int32),
            pltpu.VMEM((rows, width), jnp.bfloat16),
            pltpu.SemaphoreType.DMA((n + 2,)),
        ],
        compiler_params=pltpu.CompilerParams(vmem_limit_bytes=FULL),
        cost_estimate=pl.CostEstimate(flops=2 * rows * width * width, bytes_accessed=6 * rows * width, transcendentals=0),
        name="normalize",
    )(listed, panel, unit)


def load_kernel(tile, out, came):
    x = pltpu.make_async_copy(tile, out, came)
    x.start()
    x.wait()


def load(tile):
    return pl.pallas_call(
        load_kernel,
        out_shape=jax.ShapeDtypeStruct(tile.shape, tile.dtype),
        in_specs=[whole(pltpu.HBM)],
        out_specs=whole(VMEM),
        scratch_shapes=[pltpu.SemaphoreType.DMA],
        compiler_params=pltpu.CompilerParams(vmem_limit_bytes=LIMIT),
        cost_estimate=pl.CostEstimate(flops=0, bytes_accessed=4 * tile.shape[0] * tile.shape[1], transcendentals=0),
        name="load",
    )(tile)


def pick_kernel(n, q, *refs):
    ins, outs = refs[:n], refs[n:]
    at = lax.axis_index("prow") ^ (lax.axis_index("pcol") // q)
    for b in range(n):

        @pl.when(at == b)
        def _():
            for m in range(n):
                outs[m][...] = ins[b ^ m][...]


def pick(n, q, pieces):
    shape = pieces[0].shape
    return pl.pallas_call(
        functools.partial(pick_kernel, n, q),
        out_shape=[jax.ShapeDtypeStruct(shape, jnp.bfloat16)] * n,
        in_specs=[whole(VMEM)] * n,
        out_specs=[whole(VMEM)] * n,
        compiler_params=pltpu.CompilerParams(vmem_limit_bytes=LIMIT),
        cost_estimate=pl.CostEstimate(flops=0, bytes_accessed=4 * n * shape[0] * shape[1], transcendentals=0),
        name="pick",
    )(*pieces)


def partial_kernel(n, q, halves, step, *refs):
    ins, tiles = refs[:n], refs[n : n + q]
    outs, held = refs[n + q : -1], refs[-1]
    p = lax.axis_index("prow")
    core = lax.axis_index("pcol") % q
    chunks, part, width = ins[0].shape
    for a in range(n):
        for k in range(chunks):
            held[pl.ds(pl.multiple_of((a ^ p) * part, part), part), k * width : (k + 1) * width] = ins[a][k]
    rows, depth = tiles[0].shape
    tall = rows // HALVES
    for i, h in enumerate(halves):
        for r in range(tall // step):
            base = h * tall + r * step
            total = None
            for e in range(q):
                right = held[pl.ds(pl.multiple_of((core ^ e) * depth, depth), depth), :]
                term = jnp.dot(tiles[e][base : base + step, :], right, preferred_element_type=jnp.float32)
                total = term if total is None else total + term
            for k in range(chunks):
                outs[k * len(halves) + i][r * step : (r + 1) * step, :] = total[:, k * width : (k + 1) * width].astype(
                    jnp.bfloat16
                )


def partial_product(n, q, halves, pieces, tiles):
    chunks, part, width = pieces[0].shape
    rows, depth = tiles[0].shape
    tall = rows // HALVES
    outs = pl.pallas_call(
        functools.partial(partial_kernel, n, q, halves, min(tall, 512)),
        out_shape=[jax.ShapeDtypeStruct((tall, width), jnp.bfloat16)] * (chunks * len(halves)),
        in_specs=[whole(VMEM)] * (n + q),
        out_specs=[whole(VMEM)] * (chunks * len(halves)),
        scratch_shapes=[pltpu.VMEM((n * part, chunks * width), jnp.bfloat16)],
        compiler_params=pltpu.CompilerParams(vmem_limit_bytes=LIMIT),
        cost_estimate=pl.CostEstimate(
            flops=2 * tall * len(halves) * width * chunks * depth * q,
            bytes_accessed=2 * q * tall * len(halves) * depth,
            transcendentals=0,
        ),
        name="partial_product",
    )(*pieces, *tiles)
    return [list(outs[k * len(halves) : (k + 1) * len(halves)]) for k in range(chunks)]


def piece_kernel(n, q, which, base, step, *refs):
    ins, tiles = refs[: len(which)], refs[len(which) : len(which) + q]
    before, out = refs[len(which) + q : -1], refs[-1]
    p = lax.axis_index("prow")
    core = lax.axis_index("pcol") % q
    _, part, _ = ins[0].shape
    each = n // q
    for r in range(out.shape[0] // step):
        here = slice(r * step, (r + 1) * step)
        there = slice(base + r * step, base + (r + 1) * step)
        total = before[0][there, :] if before else None
        for a, piece in zip(which, ins):
            g = a ^ p
            columns = pl.ds(pl.multiple_of((g % each) * part, part), part)
            left = tiles[0][there, columns]
            for e in range(1, q):
                left = jnp.where((core ^ e) == g // each, tiles[e][there, columns], left)
            term = jnp.dot(left, piece[0], preferred_element_type=jnp.float32)
            total = term if total is None else total + term
        out[here, :] = total.astype(out.dtype)


def piece_product(n, q, which, pieces, tiles, base, tall, before, dtype):
    _, part, width = pieces[0].shape
    return pl.pallas_call(
        functools.partial(piece_kernel, n, q, which, base, min(tall, 512)),
        out_shape=jax.ShapeDtypeStruct((tall, width), dtype),
        in_specs=[whole(VMEM)] * (len(which) + q + len(before)),
        out_specs=whole(VMEM),
        compiler_params=pltpu.CompilerParams(vmem_limit_bytes=LIMIT),
        cost_estimate=pl.CostEstimate(
            flops=2 * tall * width * part * len(which), bytes_accessed=2 * tall * part * len(which), transcendentals=0
        ),
        name="piece_product",
    )(*pieces, *tiles, *before)


def among(z, planes):
    return functools.reduce(jnp.logical_or, [z == y for y in planes])


def add_kernel(n, q, planes, x, y, out):
    z = lax.axis_index("pcol") // q
    total = x[...].astype(jnp.float32) + y[...].astype(jnp.float32)
    if len(planes) < n:
        total = jnp.where(among(z, planes), total, x[...].astype(jnp.float32))
    out[...] = total.astype(out.dtype)


def add(n, q, x, came):
    if came is None:
        return x
    y, planes = came
    return pl.pallas_call(
        functools.partial(add_kernel, n, q, planes),
        out_shape=jax.ShapeDtypeStruct(x.shape, x.dtype),
        in_specs=[whole(VMEM)] * 2,
        out_specs=whole(VMEM),
        compiler_params=pltpu.CompilerParams(vmem_limit_bytes=LIMIT),
        cost_estimate=pl.CostEstimate(flops=x.size, bytes_accessed=6 * x.size, transcendentals=0),
        name="add",
    )(x, y)


def ahead_kernel(*refs):
    loads, rows, out = refs[:HALVES], refs[HALVES : 2 * HALVES], refs[-1]
    tall = loads[0].shape[0]
    step = min(tall, 512)
    total = None
    for load, right in zip(loads, rows):
        for r in range(tall // step):
            here = slice(r * step, (r + 1) * step)
            left = load[here, :].astype(jnp.float32).T.astype(jnp.bfloat16)
            term = jnp.dot(left, right[here, :], preferred_element_type=jnp.float32)
            total = term if total is None else total + term
    out[...] = total.astype(out.dtype)


def ahead(loads, rows, dtype):
    tall, width = loads[0].shape
    return pl.pallas_call(
        ahead_kernel,
        out_shape=jax.ShapeDtypeStruct((width, width), dtype),
        in_specs=[whole(VMEM)] * (2 * HALVES),
        out_specs=whole(VMEM),
        compiler_params=pltpu.CompilerParams(vmem_limit_bytes=LIMIT),
        cost_estimate=pl.CostEstimate(
            flops=2 * HALVES * tall * width * width, bytes_accessed=4 * HALVES * tall * width, transcendentals=0
        ),
        name="ahead",
    )(*loads, *rows)


def chosen_planes(n, q, planes):
    z = lax.axis_index("pcol") // q
    return [None if len(at) == n else among(z, at) for at in planes]


def gathered_kernel(n, q, planes, diag, *refs):
    early, total, sent = refs[:-2], refs[-2], refs[-1]
    x = diag[...]
    for y, take in zip(early, chosen_planes(n, q, planes)):
        y = y[...].astype(jnp.float32)
        x = x + (y if take is None else jnp.where(take, y, 0.0))
    total[...] = x
    sent[...] = x.astype(jnp.bfloat16)


def gathered(n, q, planes, diag, early):
    return pl.pallas_call(
        functools.partial(gathered_kernel, n, q, planes),
        out_shape=[jax.ShapeDtypeStruct(diag.shape, jnp.float32), jax.ShapeDtypeStruct(diag.shape, jnp.bfloat16)],
        in_specs=[whole(VMEM)] * (1 + len(early)),
        out_specs=[whole(VMEM)] * 2,
        compiler_params=pltpu.CompilerParams(vmem_limit_bytes=LIMIT),
        cost_estimate=pl.CostEstimate(flops=4 * diag.size, bytes_accessed=16 * diag.size, transcendentals=0),
        name="gathered",
    )(diag, *early)


def masked_kernel(n, q, planes, rows, h, count, listed, *refs):
    parts, off = refs[:count], refs[-1]
    p = lax.axis_index("prow")
    c = lax.axis_index("pcol")
    takes = chosen_planes(n, q, planes)
    per = off.shape[1] // BLOCK
    base = p * (rows // BLOCK) + (h * pl.num_programs(0) + pl.program_id(0)) * per
    x = parts[0][...].astype(jnp.float32)
    for y, take in zip(parts[1:], takes):
        y = y[...].astype(jnp.float32)
        x = x + (y if take is None else jnp.where(take, y, 0.0))
    x = x.T
    for b in range(per):
        keep = listed[c, base + b].astype(jnp.float32)
        off[:, b * BLOCK : (b + 1) * BLOCK] = -(x[:, b * BLOCK : (b + 1) * BLOCK] * keep)


def masked(n, q, planes, rows, h, listed, parts, before):
    tall, width = parts[0].shape
    step = min(tall, 512)
    count = tall // step
    return pl.pallas_call(
        functools.partial(masked_kernel, n, q, planes, rows, h, len(parts)),
        grid=(count,),
        out_shape=jax.ShapeDtypeStruct((width, rows), jnp.float32),
        in_specs=[whole(SMEM)] + [pl.BlockSpec((step, width), lambda i: (i, 0))] * len(parts) + [whole(pl.ANY)] * len(before),
        out_specs=pl.BlockSpec((width, step), lambda i: (0, h * count + i)),
        input_output_aliases={1 + len(parts): 0} if before else {},
        compiler_params=pltpu.CompilerParams(vmem_limit_bytes=LIMIT),
        cost_estimate=pl.CostEstimate(flops=4 * tall * width, bytes_accessed=10 * tall * width, transcendentals=0),
        name="masked",
    )(listed, *parts, *before)


def per_device(n, ncol, l_panel, inverse_tile, unit_inverse, pivot_inverse, listed):
    return level(n, ncol, l_panel, inverse_tile, unit_inverse, pivot_inverse, listed)


def level(n, ncol, l_panel, inverse_tile, unit_inverse, pivot_inverse, listed):
    q = ncol // n
    devices = [(p, z, k) for p in range(n) for z in range(n) for k in range(q)]

    def at(p, z, k):
        return p * ncol + z * q + k

    def swap(x, move):
        pairs = []
        for d in devices:
            to = move(*d)
            if to is not None:
                pairs.append((at(*d), at(*to)))
        return lax.ppermute(x, AXES, pairs)

    def over_rows(x, a):
        return swap(x, lambda p, z, k: (p ^ a, z, k))

    made = normalize(n, listed, l_panel, unit_inverse)
    pieces, lhat = made[:n], made[n:]
    tiles = [load(inverse_tile)]
    tiles += [swap(inverse_tile, lambda p, z, k: (p, z, k ^ e)) for e in range(1, q)]
    tiles = [pltpu.with_memory_space_constraint(t, pltpu.VMEM) for t in tiles]

    def line_swap(x, odd, d):
        to = {}
        for z in line_pairs(n, d, odd):
            to[z], to[z + 1] = z + 1, z
        got = swap(x, lambda p, z, k: (p, to[z], k) if z in to else (p, z, k ^ (q > 1)))
        return got, tuple(sorted(to))

    sides = [odd for odd in (0, 1) if line_pairs(n, 1, odd)]
    theirs = {odd: [line_swap(lhat[h], odd, 1)[0] for h in range(HALVES)] for odd in sides}

    scattered = [pieces[0]] + [over_rows(pieces[a], a) for a in range(1, n)]
    chosen = pick(n, q, scattered)

    mine = [chosen[0]] + [swap(chosen[m], lambda p, z, k: (p, z ^ m, k)) for m in range(1, n)]
    chunk = [None] * n
    for i, group in enumerate(groups(n)):
        load_ = jnp.stack([mine[m] for m in group])
        quarters = [load_] + [over_rows(load_, a) for a in range(1, n)]
        if i == 1:
            rows = inverse_tile.shape[0]
            most = piece_product(n, q, range(n - 1), quarters[:-1], tiles, 0, rows, [], jnp.float32)
            chunk[group[0]] = []
            for h in range(HALVES):
                tall = rows // HALVES
                x = piece_product(n, q, [n - 1], quarters[-1:], tiles, h * tall, tall, [most], jnp.bfloat16)
                chunk[group[0]].append(x)
        else:
            done = partial_product(n, q, tuple(range(HALVES)), quarters, tiles)
            for m, x in zip(group, done):
                chunk[m] = x

    z_here = lax.axis_index("pcol") // q

    def own(odd, d, h):
        at_mask = {}
        for z in range(n):
            to = z + d if (z % 2) == odd else z - d
            if 0 <= to < n:
                at_mask.setdefault(z ^ to, []).append(z)
        masks = sorted(at_mask)
        x = chunk[masks[0]][h]
        for m in masks[1:]:
            here = functools.reduce(jnp.logical_or, [z_here == z for z in at_mask[m]])
            x = jnp.where(here, chunk[m][h], x)
        return x

    early, loads = [], ([], [])
    came = [[None, None] for _ in range(HALVES)]
    for d in range(n - 1, 0, -1):
        for h in range(HALVES):
            sent = [None, None]
            for odd in (0, 1):
                if not line_pairs(n, d, odd):
                    continue
                load_ = add(n, q, own(odd, d, h), came[h][1 - odd])
                sent[odd] = line_swap(load_, odd, d)
                loads[odd].append(load_)
                if d == 1 and h == HALVES - 1:
                    term = ahead(loads[odd][-HALVES:], theirs[odd], jnp.bfloat16)
                    early.append(line_swap(term, odd, d)[0])
            came[h] = sent

    parts = [[chunk[0][h]] + [x[0] for x in came[h] if x is not None] for h in range(HALVES)]
    planes = [x[1] for x in came[0] if x is not None]
    part = ahead(chunk[0], lhat, jnp.float32)
    part, travel = gathered(n, q, planes, part, early)
    off = []
    for h in range(HALVES):
        off = [masked(n, q, planes, inverse_tile.shape[0], h, listed, parts[h], off)]
    total = part
    for a in range(1, n):
        total = total + over_rows(travel, a).astype(jnp.float32)
    return off[0], pivot_inverse + total[None]


def groups(n):
    return [[0], [n - 1]] + [[m] for m in range(n - 2, 0, -1)]


def line_pairs(n, d, odd):
    return [z for z in range(odd, n - 1, 2) if z + d < n or z + 1 - d >= 0]


def solution(mesh):
    n, ncol = mesh.shape["prow"], mesh.shape["pcol"]
    return jax.shard_map(
        functools.partial(per_device, n, ncol),
        mesh=mesh,
        in_specs=(
            P("prow", "pcol"),
            P("prow", "pcol"),
            P("pcol", None, None),
            P("pcol", None, None),
            P(),
        ),
        out_specs=(P("pcol", "prow"), P("pcol", None, None)),
        check_vma=False,
    )
```

```python
import functools

import jax
import jax.numpy as jnp
from jax import lax
from jax.experimental import pallas as pl
from jax.experimental.pallas import tpu as pltpu
from jax.sharding import PartitionSpec as P


BLOCK = 128
AXES = ("prow", "pcol")
VMEM = pltpu.VMEM
SMEM = pltpu.SMEM
LIMIT = 24 << 20
HALVES = 2


def whole(space):
    return pl.BlockSpec(memory_space=space)


def normalize_kernel(n, listed, panel, unit, *refs):
    outs, (rows, right, keeps, ordered, came) = refs[:-5], refs[-5:]
    p = lax.axis_index("prow")
    c = lax.axis_index("pcol")
    part = panel.shape[0] // n
    per = part // BLOCK
    order = list(range(1, n)) + [0]
    first = [
        pltpu.make_async_copy(unit.at[0], right, came.at[n]),
        pltpu.make_async_copy(listed.at[pl.ds(c, 1), :], keeps, came.at[n + 1]),
    ]
    take = [
        pltpu.make_async_copy(panel.at[pl.ds(pl.multiple_of((p ^ a) * part, part), part), :], rows.at[a], came.at[a])
        for a in order
    ]
    for x in first + take:
        x.start()
    for x in first:
        x.wait()
    for a, x in zip(order, take):
        x.wait()
        g = p ^ a
        t = jnp.dot(rows[a], right[...], preferred_element_type=jnp.float32)
        for b in range(per):
            keep = keeps[0, (p * n + g) * per + b].astype(jnp.float32)
            v = (t[b * BLOCK : (b + 1) * BLOCK] * keep).astype(jnp.bfloat16)
            outs[a][b * BLOCK : (b + 1) * BLOCK, :] = v
            ordered[pl.ds(pl.multiple_of(g * part + b * BLOCK, BLOCK), BLOCK), :] = v
    tall = panel.shape[0] // HALVES
    for h in range(HALVES):
        outs[n + h][...] = ordered[h * tall : (h + 1) * tall, :]


def normalize(n, listed, panel, unit):
    rows, width = panel.shape
    part = rows // n
    shapes = [jax.ShapeDtypeStruct((part, width), jnp.bfloat16)] * n + [
        jax.ShapeDtypeStruct((rows // HALVES, width), jnp.bfloat16)
    ] * HALVES
    return pl.pallas_call(
        functools.partial(normalize_kernel, n),
        out_shape=shapes,
        in_specs=[whole(pltpu.HBM)] * 3,
        out_specs=[whole(VMEM)] * (n + HALVES),
        scratch_shapes=[
            pltpu.VMEM((n, part, width), jnp.bfloat16),
            pltpu.VMEM((width, width), jnp.bfloat16),
            pltpu.SMEM((1, listed.shape[1]), jnp.int32),
            pltpu.VMEM((rows, width), jnp.bfloat16),
            pltpu.SemaphoreType.DMA((n + 2,)),
        ],
        compiler_params=pltpu.CompilerParams(vmem_limit_bytes=LIMIT),
        cost_estimate=pl.CostEstimate(flops=2 * rows * width * width, bytes_accessed=6 * rows * width, transcendentals=0),
        name="normalize",
    )(listed, panel, unit)


def load_kernel(tile, out, came):
    x = pltpu.make_async_copy(tile, out, came)
    x.start()
    x.wait()


def load(tile):
    return pl.pallas_call(
        load_kernel,
        out_shape=jax.ShapeDtypeStruct(tile.shape, tile.dtype),
        in_specs=[whole(pltpu.HBM)],
        out_specs=whole(VMEM),
        scratch_shapes=[pltpu.SemaphoreType.DMA],
        compiler_params=pltpu.CompilerParams(vmem_limit_bytes=LIMIT),
        cost_estimate=pl.CostEstimate(flops=0, bytes_accessed=4 * tile.shape[0] * tile.shape[1], transcendentals=0),
        name="load",
    )(tile)


def pick_kernel(n, q, *refs):
    ins, outs = refs[:n], refs[n:]
    at = lax.axis_index("prow") ^ (lax.axis_index("pcol") // q)
    for b in range(n):

        @pl.when(at == b)
        def _():
            for m in range(n):
                outs[m][...] = ins[b ^ m][...]


def pick(n, q, pieces):
    shape = pieces[0].shape
    return pl.pallas_call(
        functools.partial(pick_kernel, n, q),
        out_shape=[jax.ShapeDtypeStruct(shape, jnp.bfloat16)] * n,
        in_specs=[whole(VMEM)] * n,
        out_specs=[whole(VMEM)] * n,
        compiler_params=pltpu.CompilerParams(vmem_limit_bytes=LIMIT),
        cost_estimate=pl.CostEstimate(flops=0, bytes_accessed=4 * n * shape[0] * shape[1], transcendentals=0),
        name="pick",
    )(*pieces)


def partial_kernel(n, q, halves, step, *refs):
    ins, tiles = refs[:n], refs[n : n + q]
    outs, held = refs[n + q : -1], refs[-1]
    p = lax.axis_index("prow")
    core = lax.axis_index("pcol") % q
    chunks, part, width = ins[0].shape
    for a in range(n):
        for k in range(chunks):
            held[pl.ds(pl.multiple_of((a ^ p) * part, part), part), k * width : (k + 1) * width] = ins[a][k]
    rows, depth = tiles[0].shape
    tall = rows // HALVES
    for i, h in enumerate(halves):
        for r in range(tall // step):
            base = h * tall + r * step
            total = None
            for e in range(q):
                right = held[pl.ds(pl.multiple_of((core ^ e) * depth, depth), depth), :]
                term = jnp.dot(tiles[e][base : base + step, :], right, preferred_element_type=jnp.float32)
                total = term if total is None else total + term
            for k in range(chunks):
                outs[k * len(halves) + i][r * step : (r + 1) * step, :] = total[:, k * width : (k + 1) * width].astype(
                    jnp.bfloat16
                )


def partial_product(n, q, halves, pieces, tiles):
    chunks, part, width = pieces[0].shape
    rows, depth = tiles[0].shape
    tall = rows // HALVES
    outs = pl.pallas_call(
        functools.partial(partial_kernel, n, q, halves, min(tall, 512)),
        out_shape=[jax.ShapeDtypeStruct((tall, width), jnp.bfloat16)] * (chunks * len(halves)),
        in_specs=[whole(VMEM)] * (n + q),
        out_specs=[whole(VMEM)] * (chunks * len(halves)),
        scratch_shapes=[pltpu.VMEM((n * part, chunks * width), jnp.bfloat16)],
        compiler_params=pltpu.CompilerParams(vmem_limit_bytes=LIMIT),
        cost_estimate=pl.CostEstimate(
            flops=2 * tall * len(halves) * width * chunks * depth * q,
            bytes_accessed=2 * q * tall * len(halves) * depth,
            transcendentals=0,
        ),
        name="partial_product",
    )(*pieces, *tiles)
    return [list(outs[k * len(halves) : (k + 1) * len(halves)]) for k in range(chunks)]


def piece_kernel(n, q, which, base, step, *refs):
    ins, tiles = refs[: len(which)], refs[len(which) : len(which) + q]
    before, out = refs[len(which) + q : -1], refs[-1]
    p = lax.axis_index("prow")
    core = lax.axis_index("pcol") % q
    _, part, _ = ins[0].shape
    each = n // q
    for r in range(out.shape[0] // step):
        here = slice(r * step, (r + 1) * step)
        there = slice(base + r * step, base + (r + 1) * step)
        total = before[0][there, :] if before else None
        for a, piece in zip(which, ins):
            g = a ^ p
            columns = pl.ds(pl.multiple_of((g % each) * part, part), part)
            left = tiles[0][there, columns]
            for e in range(1, q):
                left = jnp.where((core ^ e) == g // each, tiles[e][there, columns], left)
            term = jnp.dot(left, piece[0], preferred_element_type=jnp.float32)
            total = term if total is None else total + term
        out[here, :] = total.astype(out.dtype)


def piece_product(n, q, which, pieces, tiles, base, tall, before, dtype):
    _, part, width = pieces[0].shape
    return pl.pallas_call(
        functools.partial(piece_kernel, n, q, which, base, min(tall, 512)),
        out_shape=jax.ShapeDtypeStruct((tall, width), dtype),
        in_specs=[whole(VMEM)] * (len(which) + q + len(before)),
        out_specs=whole(VMEM),
        compiler_params=pltpu.CompilerParams(vmem_limit_bytes=LIMIT),
        cost_estimate=pl.CostEstimate(
            flops=2 * tall * width * part * len(which), bytes_accessed=2 * tall * part * len(which), transcendentals=0
        ),
        name="piece_product",
    )(*pieces, *tiles, *before)


def among(z, planes):
    return functools.reduce(jnp.logical_or, [z == y for y in planes])


def add_kernel(n, q, planes, x, y, out):
    z = lax.axis_index("pcol") // q
    total = x[...].astype(jnp.float32) + y[...].astype(jnp.float32)
    if len(planes) < n:
        total = jnp.where(among(z, planes), total, x[...].astype(jnp.float32))
    out[...] = total.astype(out.dtype)


def add(n, q, x, came):
    if came is None:
        return x
    y, planes = came
    return pl.pallas_call(
        functools.partial(add_kernel, n, q, planes),
        out_shape=jax.ShapeDtypeStruct(x.shape, x.dtype),
        in_specs=[whole(VMEM)] * 2,
        out_specs=whole(VMEM),
        compiler_params=pltpu.CompilerParams(vmem_limit_bytes=LIMIT),
        cost_estimate=pl.CostEstimate(flops=x.size, bytes_accessed=6 * x.size, transcendentals=0),
        name="add",
    )(x, y)


def ahead_kernel(*refs):
    loads, rows, out = refs[:HALVES], refs[HALVES : 2 * HALVES], refs[-1]
    tall = loads[0].shape[0]
    step = min(tall, 512)
    total = None
    for load, right in zip(loads, rows):
        for r in range(tall // step):
            here = slice(r * step, (r + 1) * step)
            left = load[here, :].astype(jnp.float32).T.astype(jnp.bfloat16)
            term = jnp.dot(left, right[here, :], preferred_element_type=jnp.float32)
            total = term if total is None else total + term
    out[...] = total.astype(out.dtype)


def ahead(loads, rows, dtype):
    tall, width = loads[0].shape
    return pl.pallas_call(
        ahead_kernel,
        out_shape=jax.ShapeDtypeStruct((width, width), dtype),
        in_specs=[whole(VMEM)] * (2 * HALVES),
        out_specs=whole(VMEM),
        compiler_params=pltpu.CompilerParams(vmem_limit_bytes=LIMIT),
        cost_estimate=pl.CostEstimate(
            flops=2 * HALVES * tall * width * width, bytes_accessed=4 * HALVES * tall * width, transcendentals=0
        ),
        name="ahead",
    )(*loads, *rows)


def chosen_planes(n, q, planes):
    z = lax.axis_index("pcol") // q
    return [None if len(at) == n else among(z, at) for at in planes]


def gathered_kernel(n, q, planes, diag, *refs):
    early, total, sent = refs[:-2], refs[-2], refs[-1]
    x = diag[...]
    for y, take in zip(early, chosen_planes(n, q, planes)):
        y = y[...].astype(jnp.float32)
        x = x + (y if take is None else jnp.where(take, y, 0.0))
    total[...] = x
    sent[...] = x.astype(jnp.bfloat16)


def gathered(n, q, planes, diag, early):
    return pl.pallas_call(
        functools.partial(gathered_kernel, n, q, planes),
        out_shape=[jax.ShapeDtypeStruct(diag.shape, jnp.float32), jax.ShapeDtypeStruct(diag.shape, jnp.bfloat16)],
        in_specs=[whole(VMEM)] * (1 + len(early)),
        out_specs=[whole(VMEM)] * 2,
        compiler_params=pltpu.CompilerParams(vmem_limit_bytes=LIMIT),
        cost_estimate=pl.CostEstimate(flops=4 * diag.size, bytes_accessed=16 * diag.size, transcendentals=0),
        name="gathered",
    )(diag, *early)


def masked_kernel(n, q, planes, rows, h, count, listed, *refs):
    parts, off = refs[:count], refs[-1]
    p = lax.axis_index("prow")
    c = lax.axis_index("pcol")
    takes = chosen_planes(n, q, planes)
    per = off.shape[1] // BLOCK
    base = p * (rows // BLOCK) + (h * pl.num_programs(0) + pl.program_id(0)) * per
    x = parts[0][...].astype(jnp.float32)
    for y, take in zip(parts[1:], takes):
        y = y[...].astype(jnp.float32)
        x = x + (y if take is None else jnp.where(take, y, 0.0))
    x = x.T
    for b in range(per):
        keep = listed[c, base + b].astype(jnp.float32)
        off[:, b * BLOCK : (b + 1) * BLOCK] = -(x[:, b * BLOCK : (b + 1) * BLOCK] * keep)


def masked(n, q, planes, rows, h, listed, parts, before):
    tall, width = parts[0].shape
    step = min(tall, 1024)
    count = tall // step
    return pl.pallas_call(
        functools.partial(masked_kernel, n, q, planes, rows, h, len(parts)),
        grid=(count,),
        out_shape=jax.ShapeDtypeStruct((width, rows), jnp.float32),
        in_specs=[whole(SMEM)] + [pl.BlockSpec((step, width), lambda i: (i, 0))] * len(parts) + [whole(pl.ANY)] * len(before),
        out_specs=pl.BlockSpec((width, step), lambda i: (0, h * count + i)),
        input_output_aliases={1 + len(parts): 0} if before else {},
        compiler_params=pltpu.CompilerParams(vmem_limit_bytes=LIMIT),
        cost_estimate=pl.CostEstimate(flops=4 * tall * width, bytes_accessed=10 * tall * width, transcendentals=0),
        name="masked",
    )(listed, *parts, *before)


def per_device(n, ncol, l_panel, inverse_tile, unit_inverse, pivot_inverse, listed):
    return level(n, ncol, l_panel, inverse_tile, unit_inverse, pivot_inverse, listed)


def level(n, ncol, l_panel, inverse_tile, unit_inverse, pivot_inverse, listed):
    q = ncol // n
    devices = [(p, z, k) for p in range(n) for z in range(n) for k in range(q)]

    def at(p, z, k):
        return p * ncol + z * q + k

    def swap(x, move):
        pairs = []
        for d in devices:
            to = move(*d)
            if to is not None:
                pairs.append((at(*d), at(*to)))
        return lax.ppermute(x, AXES, pairs)

    def over_rows(x, a):
        return swap(x, lambda p, z, k: (p ^ a, z, k))

    made = normalize(n, *[pltpu.with_memory_space_constraint(x, pltpu.HBM) for x in (listed, l_panel, unit_inverse)])
    pieces, lhat = made[:n], made[n:]
    tiles = [load(inverse_tile)]
    tiles += [swap(inverse_tile, lambda p, z, k: (p, z, k ^ e)) for e in range(1, q)]
    tiles = [pltpu.with_memory_space_constraint(t, pltpu.VMEM) for t in tiles]

    def line_swap(x, odd, d):
        to = {}
        for z in line_pairs(n, d, odd):
            to[z], to[z + 1] = z + 1, z
        got = swap(x, lambda p, z, k: (p, to[z], k) if z in to else (p, z, k ^ (q > 1)))
        return got, tuple(sorted(to))

    sides = [odd for odd in (0, 1) if line_pairs(n, 1, odd)]
    theirs = {odd: [line_swap(lhat[h], odd, 1)[0] for h in range(HALVES)] for odd in sides}

    scattered = [pieces[0]] + [over_rows(pieces[a], a) for a in range(1, n)]
    chosen = pick(n, q, scattered)

    mine = [chosen[0]] + [swap(chosen[m], lambda p, z, k: (p, z ^ m, k)) for m in range(1, n)]
    chunk = [None] * n
    for i, group in enumerate(groups(n)):
        load_ = jnp.stack([mine[m] for m in group])
        quarters = [load_] + [over_rows(load_, a) for a in range(1, n)]
        if i == 1:
            rows = inverse_tile.shape[0]
            most = piece_product(n, q, range(n - 1), quarters[:-1], tiles, 0, rows, [], jnp.float32)
            chunk[group[0]] = []
            for h in range(HALVES):
                tall = rows // HALVES
                x = piece_product(n, q, [n - 1], quarters[-1:], tiles, h * tall, tall, [most], jnp.bfloat16)
                chunk[group[0]].append(x)
        else:
            done = partial_product(n, q, tuple(range(HALVES)), quarters, tiles)
            for m, x in zip(group, done):
                chunk[m] = x

    z_here = lax.axis_index("pcol") // q

    def own(odd, d, h):
        at_mask = {}
        for z in range(n):
            to = z + d if (z % 2) == odd else z - d
            if 0 <= to < n:
                at_mask.setdefault(z ^ to, []).append(z)
        masks = sorted(at_mask)
        x = chunk[masks[0]][h]
        for m in masks[1:]:
            here = functools.reduce(jnp.logical_or, [z_here == z for z in at_mask[m]])
            x = jnp.where(here, chunk[m][h], x)
        return x

    early, loads = [], ([], [])
    came = [[None, None] for _ in range(HALVES)]
    for d in range(n - 1, 0, -1):
        for h in range(HALVES):
            sent = [None, None]
            for odd in (0, 1):
                if not line_pairs(n, d, odd):
                    continue
                load_ = add(n, q, own(odd, d, h), came[h][1 - odd])
                sent[odd] = line_swap(load_, odd, d)
                loads[odd].append(load_)
                if d == 1 and h == HALVES - 1:
                    term = ahead(loads[odd][-HALVES:], theirs[odd], jnp.bfloat16)
                    early.append(line_swap(term, odd, d)[0])
            came[h] = sent

    parts = [[chunk[0][h]] + [x[0] for x in came[h] if x is not None] for h in range(HALVES)]
    planes = [x[1] for x in came[0] if x is not None]
    part = ahead(chunk[0], lhat, jnp.float32)
    part, travel = gathered(n, q, planes, part, early)
    off = []
    for h in range(HALVES):
        off = [masked(n, q, planes, inverse_tile.shape[0], h, listed, parts[h], off)]
    total = part
    for a in range(1, n):
        total = total + over_rows(travel, a).astype(jnp.float32)
    return off[0], pivot_inverse + total[None]


def groups(n):
    return [[0], [n - 1]] + [[m] for m in range(n - 2, 0, -1)]


def line_pairs(n, d, odd):
    return [z for z in range(odd, n - 1, 2) if z + d < n or z + 1 - d >= 0]


def solution(mesh):
    n, ncol = mesh.shape["prow"], mesh.shape["pcol"]
    return jax.shard_map(
        functools.partial(per_device, n, ncol),
        mesh=mesh,
        in_specs=(
            P("prow", "pcol"),
            P("prow", "pcol"),
            P("pcol", None, None),
            P("pcol", None, None),
            P(),
        ),
        out_specs=(P("pcol", "prow"), P("pcol", None, None)),
        check_vma=False,
    )
```

```python
import functools

import jax
import jax.numpy as jnp
from jax import lax
from jax.experimental import pallas as pl
from jax.experimental.pallas import tpu as pltpu
from jax.sharding import PartitionSpec as P


BLOCK = 128
AXES = ("prow", "pcol")
VMEM = pltpu.VMEM
SMEM = pltpu.SMEM
LIMIT = 24 << 20
HALVES = 2


def whole(space):
    return pl.BlockSpec(memory_space=space)


def normalize_kernel(n, listed, panel, unit, *refs):
    outs, (rows, right, keeps, ordered, came) = refs[:-5], refs[-5:]
    p = lax.axis_index("prow")
    c = lax.axis_index("pcol")
    part = panel.shape[0] // n
    per = part // BLOCK
    order = list(range(1, n)) + [0]
    first = [
        pltpu.make_async_copy(unit.at[0], right, came.at[n]),
        pltpu.make_async_copy(listed.at[pl.ds(c, 1), :], keeps, came.at[n + 1]),
    ]
    take = [
        pltpu.make_async_copy(panel.at[pl.ds(pl.multiple_of((p ^ a) * part, part), part), :], rows.at[a], came.at[a])
        for a in order
    ]
    for x in first + take:
        x.start()
    for x in first:
        x.wait()
    for a, x in zip(order, take):
        x.wait()
        g = p ^ a
        t = jnp.dot(rows[a], right[...], preferred_element_type=jnp.float32)
        for b in range(per):
            keep = keeps[0, (p * n + g) * per + b].astype(jnp.float32)
            v = (t[b * BLOCK : (b + 1) * BLOCK] * keep).astype(jnp.bfloat16)
            outs[a][b * BLOCK : (b + 1) * BLOCK, :] = v
            ordered[pl.ds(pl.multiple_of(g * part + b * BLOCK, BLOCK), BLOCK), :] = v
    tall = panel.shape[0] // HALVES
    for h in range(HALVES):
        outs[n + h][...] = ordered[h * tall : (h + 1) * tall, :]


def normalize(n, listed, panel, unit):
    rows, width = panel.shape
    part = rows // n
    shapes = [jax.ShapeDtypeStruct((part, width), jnp.bfloat16)] * n + [
        jax.ShapeDtypeStruct((rows // HALVES, width), jnp.bfloat16)
    ] * HALVES
    return pl.pallas_call(
        functools.partial(normalize_kernel, n),
        out_shape=shapes,
        in_specs=[whole(pltpu.HBM)] * 3,
        out_specs=[whole(VMEM)] * (n + HALVES),
        scratch_shapes=[
            pltpu.VMEM((n, part, width), jnp.bfloat16),
            pltpu.VMEM((width, width), jnp.bfloat16),
            pltpu.SMEM((1, listed.shape[1]), jnp.int32),
            pltpu.VMEM((rows, width), jnp.bfloat16),
            pltpu.SemaphoreType.DMA((n + 2,)),
        ],
        compiler_params=pltpu.CompilerParams(vmem_limit_bytes=LIMIT),
        cost_estimate=pl.CostEstimate(flops=2 * rows * width * width, bytes_accessed=6 * rows * width, transcendentals=0),
        name="normalize",
    )(listed, panel, unit)


def load_kernel(tile, out, came):
    x = pltpu.make_async_copy(tile, out, came)
    x.start()
    x.wait()


def load(tile):
    return pl.pallas_call(
        load_kernel,
        out_shape=jax.ShapeDtypeStruct(tile.shape, tile.dtype),
        in_specs=[whole(pltpu.HBM)],
        out_specs=whole(VMEM),
        scratch_shapes=[pltpu.SemaphoreType.DMA],
        compiler_params=pltpu.CompilerParams(vmem_limit_bytes=LIMIT),
        cost_estimate=pl.CostEstimate(flops=0, bytes_accessed=4 * tile.shape[0] * tile.shape[1], transcendentals=0),
        name="load",
    )(tile)


def pick_kernel(n, q, *refs):
    ins, outs = refs[:n], refs[n:]
    at = lax.axis_index("prow") ^ (lax.axis_index("pcol") // q)
    for b in range(n):

        @pl.when(at == b)
        def _():
            for m in range(n):
                outs[m][...] = ins[b ^ m][...]


def pick(n, q, pieces):
    shape = pieces[0].shape
    return pl.pallas_call(
        functools.partial(pick_kernel, n, q),
        out_shape=[jax.ShapeDtypeStruct(shape, jnp.bfloat16)] * n,
        in_specs=[whole(VMEM)] * n,
        out_specs=[whole(VMEM)] * n,
        compiler_params=pltpu.CompilerParams(vmem_limit_bytes=LIMIT),
        cost_estimate=pl.CostEstimate(flops=0, bytes_accessed=4 * n * shape[0] * shape[1], transcendentals=0),
        name="pick",
    )(*pieces)


def partial_kernel(n, q, halves, step, *refs):
    ins, tiles = refs[:n], refs[n : n + q]
    outs, held = refs[n + q : -1], refs[-1]
    p = lax.axis_index("prow")
    core = lax.axis_index("pcol") % q
    chunks, part, width = ins[0].shape
    for a in range(n):
        for k in range(chunks):
            held[pl.ds(pl.multiple_of((a ^ p) * part, part), part), k * width : (k + 1) * width] = ins[a][k]
    rows, depth = tiles[0].shape
    tall = rows // HALVES
    for i, h in enumerate(halves):
        for r in range(tall // step):
            base = h * tall + r * step
            total = None
            for e in range(q):
                right = held[pl.ds(pl.multiple_of((core ^ e) * depth, depth), depth), :]
                term = jnp.dot(tiles[e][base : base + step, :], right, preferred_element_type=jnp.float32)
                total = term if total is None else total + term
            for k in range(chunks):
                outs[k * len(halves) + i][r * step : (r + 1) * step, :] = total[:, k * width : (k + 1) * width].astype(
                    jnp.bfloat16
                )


def partial_product(n, q, halves, pieces, tiles):
    chunks, part, width = pieces[0].shape
    rows, depth = tiles[0].shape
    tall = rows // HALVES
    outs = pl.pallas_call(
        functools.partial(partial_kernel, n, q, halves, min(tall, 512)),
        out_shape=[jax.ShapeDtypeStruct((tall, width), jnp.bfloat16)] * (chunks * len(halves)),
        in_specs=[whole(VMEM)] * (n + q),
        out_specs=[whole(VMEM)] * (chunks * len(halves)),
        scratch_shapes=[pltpu.VMEM((n * part, chunks * width), jnp.bfloat16)],
        compiler_params=pltpu.CompilerParams(vmem_limit_bytes=LIMIT),
        cost_estimate=pl.CostEstimate(
            flops=2 * tall * len(halves) * width * chunks * depth * q,
            bytes_accessed=2 * q * tall * len(halves) * depth,
            transcendentals=0,
        ),
        name="partial_product",
    )(*pieces, *tiles)
    return [list(outs[k * len(halves) : (k + 1) * len(halves)]) for k in range(chunks)]


def piece_kernel(n, q, which, base, step, *refs):
    ins, tiles = refs[: len(which)], refs[len(which) : len(which) + q]
    before, out = refs[len(which) + q : -1], refs[-1]
    p = lax.axis_index("prow")
    core = lax.axis_index("pcol") % q
    _, part, _ = ins[0].shape
    each = n // q
    for r in range(out.shape[0] // step):
        here = slice(r * step, (r + 1) * step)
        there = slice(base + r * step, base + (r + 1) * step)
        total = before[0][there, :] if before else None
        for a, piece in zip(which, ins):
            g = a ^ p
            columns = pl.ds(pl.multiple_of((g % each) * part, part), part)
            left = tiles[0][there, columns]
            for e in range(1, q):
                left = jnp.where((core ^ e) == g // each, tiles[e][there, columns], left)
            term = jnp.dot(left, piece[0], preferred_element_type=jnp.float32)
            total = term if total is None else total + term
        out[here, :] = total.astype(out.dtype)


def piece_product(n, q, which, pieces, tiles, base, tall, before, dtype):
    _, part, width = pieces[0].shape
    return pl.pallas_call(
        functools.partial(piece_kernel, n, q, which, base, min(tall, 512)),
        out_shape=jax.ShapeDtypeStruct((tall, width), dtype),
        in_specs=[whole(VMEM)] * (len(which) + q + len(before)),
        out_specs=whole(VMEM),
        compiler_params=pltpu.CompilerParams(vmem_limit_bytes=LIMIT),
        cost_estimate=pl.CostEstimate(
            flops=2 * tall * width * part * len(which), bytes_accessed=2 * tall * part * len(which), transcendentals=0
        ),
        name="piece_product",
    )(*pieces, *tiles, *before)


def among(z, planes):
    return functools.reduce(jnp.logical_or, [z == y for y in planes])


def add_kernel(n, q, planes, x, y, out):
    z = lax.axis_index("pcol") // q
    total = x[...].astype(jnp.float32) + y[...].astype(jnp.float32)
    if len(planes) < n:
        total = jnp.where(among(z, planes), total, x[...].astype(jnp.float32))
    out[...] = total.astype(out.dtype)


def add(n, q, x, came):
    if came is None:
        return x
    y, planes = came
    return pl.pallas_call(
        functools.partial(add_kernel, n, q, planes),
        out_shape=jax.ShapeDtypeStruct(x.shape, x.dtype),
        in_specs=[whole(VMEM)] * 2,
        out_specs=whole(VMEM),
        compiler_params=pltpu.CompilerParams(vmem_limit_bytes=LIMIT),
        cost_estimate=pl.CostEstimate(flops=x.size, bytes_accessed=6 * x.size, transcendentals=0),
        name="add",
    )(x, y)


def ahead_kernel(*refs):
    count = len(refs) // 2
    loads, rows, out = refs[:count], refs[count:-1], refs[-1]
    tall = loads[0].shape[0]
    step = min(tall, 512)
    total = None
    for load, right in zip(loads, rows):
        for r in range(tall // step):
            here = slice(r * step, (r + 1) * step)
            left = load[here, :].astype(jnp.float32).T.astype(jnp.bfloat16)
            term = jnp.dot(left, right[here, :], preferred_element_type=jnp.float32)
            total = term if total is None else total + term
    out[...] = total.astype(out.dtype)


def ahead(loads, rows, dtype):
    tall, width = loads[0].shape
    return pl.pallas_call(
        ahead_kernel,
        out_shape=jax.ShapeDtypeStruct((width, width), dtype),
        in_specs=[whole(VMEM)] * (2 * len(loads)),
        out_specs=whole(VMEM),
        compiler_params=pltpu.CompilerParams(vmem_limit_bytes=LIMIT),
        cost_estimate=pl.CostEstimate(
            flops=2 * len(loads) * tall * width * width, bytes_accessed=4 * len(loads) * tall * width, transcendentals=0
        ),
        name="ahead",
    )(*loads, *rows)


def chosen_planes(n, q, planes):
    z = lax.axis_index("pcol") // q
    return [None if len(at) == n else among(z, at) for at in planes]


def gathered_kernel(n, q, planes, own, lhat, *refs):
    count = len(planes)
    early, came, total, sent = refs[:count], refs[count : 2 * count], refs[-2], refs[-1]
    takes = chosen_planes(n, q, planes)
    sum_ = own[...]
    for y, take in zip(early, takes):
        y = y[...].astype(jnp.float32)
        sum_ = sum_ + (y if take is None else jnp.where(take, y, 0.0))
    tall = lhat.shape[0]
    step = min(tall, 512)
    for r in range(tall // step):
        here = slice(r * step, (r + 1) * step)
        x = None
        for y, take in zip(came, takes):
            y = y[here, :].astype(jnp.float32)
            y = y if take is None else jnp.where(take, y, 0.0)
            x = y if x is None else x + y
        x = x.T
        high = x.astype(jnp.bfloat16)
        low = (x - high.astype(jnp.float32)).astype(jnp.bfloat16)
        sum_ = sum_ + jnp.dot(high, lhat[here, :], preferred_element_type=jnp.float32)
        sum_ = sum_ + jnp.dot(low, lhat[here, :], preferred_element_type=jnp.float32)
    total[...] = sum_
    sent[...] = sum_.astype(jnp.bfloat16)


def gathered(n, q, planes, own, lhat, early, came):
    tall, width = lhat.shape
    return pl.pallas_call(
        functools.partial(gathered_kernel, n, q, planes),
        out_shape=[jax.ShapeDtypeStruct(own.shape, jnp.float32), jax.ShapeDtypeStruct(own.shape, jnp.bfloat16)],
        in_specs=[whole(VMEM)] * (2 + len(early) + len(came)),
        out_specs=[whole(VMEM)] * 2,
        compiler_params=pltpu.CompilerParams(vmem_limit_bytes=LIMIT),
        cost_estimate=pl.CostEstimate(flops=4 * tall * width * width, bytes_accessed=6 * tall * width, transcendentals=0),
        name="gathered",
    )(own, lhat, *early, *came)


def masked_kernel(n, q, planes, rows, h, count, listed, *refs):
    parts, off = refs[:count], refs[-1]
    p = lax.axis_index("prow")
    c = lax.axis_index("pcol")
    takes = chosen_planes(n, q, planes)
    per = off.shape[1] // BLOCK
    base = p * (rows // BLOCK) + (h * pl.num_programs(0) + pl.program_id(0)) * per
    x = parts[0][...].astype(jnp.float32)
    for y, take in zip(parts[1:], takes):
        y = y[...].astype(jnp.float32)
        x = x + (y if take is None else jnp.where(take, y, 0.0))
    x = x.T
    for b in range(per):
        keep = listed[c, base + b].astype(jnp.float32)
        off[:, b * BLOCK : (b + 1) * BLOCK] = -(x[:, b * BLOCK : (b + 1) * BLOCK] * keep)


def masked(n, q, planes, rows, h, listed, parts, before):
    tall, width = parts[0].shape
    step = min(tall, 1024)
    count = tall // step
    return pl.pallas_call(
        functools.partial(masked_kernel, n, q, planes, rows, h, len(parts)),
        grid=(count,),
        out_shape=jax.ShapeDtypeStruct((width, rows), jnp.float32),
        in_specs=[whole(SMEM)] + [pl.BlockSpec((step, width), lambda i: (i, 0))] * len(parts) + [whole(pl.ANY)] * len(before),
        out_specs=pl.BlockSpec((width, step), lambda i: (0, h * count + i)),
        input_output_aliases={1 + len(parts): 0} if before else {},
        compiler_params=pltpu.CompilerParams(vmem_limit_bytes=LIMIT),
        cost_estimate=pl.CostEstimate(flops=4 * tall * width, bytes_accessed=10 * tall * width, transcendentals=0),
        name="masked",
    )(listed, *parts, *before)


def per_device(n, ncol, l_panel, inverse_tile, unit_inverse, pivot_inverse, listed):
    return level(n, ncol, l_panel, inverse_tile, unit_inverse, pivot_inverse, listed)


def level(n, ncol, l_panel, inverse_tile, unit_inverse, pivot_inverse, listed):
    q = ncol // n
    devices = [(p, z, k) for p in range(n) for z in range(n) for k in range(q)]

    def at(p, z, k):
        return p * ncol + z * q + k

    def swap(x, move):
        pairs = []
        for d in devices:
            to = move(*d)
            if to is not None:
                pairs.append((at(*d), at(*to)))
        return lax.ppermute(x, AXES, pairs)

    def over_rows(x, a):
        return swap(x, lambda p, z, k: (p ^ a, z, k))

    made = normalize(n, *[pltpu.with_memory_space_constraint(x, pltpu.HBM) for x in (listed, l_panel, unit_inverse)])
    pieces, lhat = made[:n], made[n:]
    tiles = [load(inverse_tile)]
    tiles += [swap(inverse_tile, lambda p, z, k: (p, z, k ^ e)) for e in range(1, q)]
    tiles = [pltpu.with_memory_space_constraint(t, pltpu.VMEM) for t in tiles]

    def line_swap(x, odd, d):
        to = {}
        for z in line_pairs(n, d, odd):
            to[z], to[z + 1] = z + 1, z
        got = swap(x, lambda p, z, k: (p, to[z], k) if z in to else (p, z, k ^ (q > 1)))
        return got, tuple(sorted(to))

    sides = [odd for odd in (0, 1) if line_pairs(n, 1, odd)]
    theirs = {odd: line_swap(lhat[-1], odd, 1)[0] for odd in sides}

    scattered = [pieces[0]] + [over_rows(pieces[a], a) for a in range(1, n)]
    chosen = pick(n, q, scattered)

    mine = [chosen[0]] + [swap(chosen[m], lambda p, z, k: (p, z ^ m, k)) for m in range(1, n)]
    chunk = [None] * n
    for i, group in enumerate(groups(n)):
        load_ = jnp.stack([mine[m] for m in group])
        quarters = [load_] + [over_rows(load_, a) for a in range(1, n)]
        if i == 1:
            rows = inverse_tile.shape[0]
            most = piece_product(n, q, range(n - 1), quarters[:-1], tiles, 0, rows, [], jnp.float32)
            chunk[group[0]] = []
            for h in range(HALVES):
                tall = rows // HALVES
                x = piece_product(n, q, [n - 1], quarters[-1:], tiles, h * tall, tall, [most], jnp.bfloat16)
                chunk[group[0]].append(x)
        else:
            done = partial_product(n, q, tuple(range(HALVES)), quarters, tiles)
            for m, x in zip(group, done):
                chunk[m] = x

    z_here = lax.axis_index("pcol") // q

    def own(odd, d, h):
        at_mask = {}
        for z in range(n):
            to = z + d if (z % 2) == odd else z - d
            if 0 <= to < n:
                at_mask.setdefault(z ^ to, []).append(z)
        masks = sorted(at_mask)
        x = chunk[masks[0]][h]
        for m in masks[1:]:
            here = functools.reduce(jnp.logical_or, [z_here == z for z in at_mask[m]])
            x = jnp.where(here, chunk[m][h], x)
        return x

    early = []
    came = [[None, None] for _ in range(HALVES)]
    for d in range(n - 1, 0, -1):
        for h in range(HALVES):
            sent = [None, None]
            for odd in (0, 1):
                if not line_pairs(n, d, odd):
                    continue
                load_ = add(n, q, own(odd, d, h), came[h][1 - odd])
                sent[odd] = line_swap(load_, odd, d)
                if d == 1 and h == HALVES - 1:
                    term = ahead([load_], [theirs[odd]], jnp.bfloat16)
                    early.append(line_swap(term, odd, d)[0])
            came[h] = sent

    parts = [[chunk[0][h]] + [x[0] for x in came[h] if x is not None] for h in range(HALVES)]
    planes = [x[1] for x in came[0] if x is not None]
    part = ahead(chunk[0], lhat, jnp.float32)
    part, travel = gathered(n, q, planes, part, lhat[0], early, parts[0][1:])
    off = []
    for h in range(HALVES):
        off = [masked(n, q, planes, inverse_tile.shape[0], h, listed, parts[h], off)]
    total = part
    for a in range(1, n):
        total = total + over_rows(travel, a).astype(jnp.float32)
    return off[0], pivot_inverse + total[None]


def groups(n):
    return [[0], [n - 1]] + [[m] for m in range(n - 2, 0, -1)]


def line_pairs(n, d, odd):
    return [z for z in range(odd, n - 1, 2) if z + d < n or z + 1 - d >= 0]


def solution(mesh):
    n, ncol = mesh.shape["prow"], mesh.shape["pcol"]
    return jax.shard_map(
        functools.partial(per_device, n, ncol),
        mesh=mesh,
        in_specs=(
            P("prow", "pcol"),
            P("prow", "pcol"),
            P("pcol", None, None),
            P("pcol", None, None),
            P(),
        ),
        out_specs=(P("pcol", "prow"), P("pcol", None, None)),
        check_vma=False,
    )
```

```python
import functools

import jax
import jax.numpy as jnp
from jax import lax
from jax.experimental import pallas as pl
from jax.experimental.pallas import tpu as pltpu
from jax.sharding import PartitionSpec as P


BLOCK = 128
AXES = ("prow", "pcol")
VMEM = pltpu.VMEM
SMEM = pltpu.SMEM
LIMIT = 24 << 20
HALVES = 2


def whole(space):
    return pl.BlockSpec(memory_space=space)


def normalize_kernel(n, listed, panel, unit, *refs):
    outs, (rows, right, keeps, ordered, came) = refs[:-5], refs[-5:]
    p = lax.axis_index("prow")
    c = lax.axis_index("pcol")
    part = panel.shape[0] // n
    per = part // BLOCK
    order = list(range(1, n)) + [0]
    first = [
        pltpu.make_async_copy(unit.at[0], right, came.at[n]),
        pltpu.make_async_copy(listed.at[pl.ds(c, 1), :], keeps, came.at[n + 1]),
    ]
    take = [
        pltpu.make_async_copy(panel.at[pl.ds(pl.multiple_of((p ^ a) * part, part), part), :], rows.at[a], came.at[a])
        for a in order
    ]
    for x in first + take:
        x.start()
    for x in first:
        x.wait()
    for a, x in zip(order, take):
        x.wait()
        g = p ^ a
        t = jnp.dot(rows[a], right[...], preferred_element_type=jnp.float32)
        for b in range(per):
            keep = keeps[0, (p * n + g) * per + b].astype(jnp.float32)
            v = (t[b * BLOCK : (b + 1) * BLOCK] * keep).astype(jnp.bfloat16)
            outs[a][b * BLOCK : (b + 1) * BLOCK, :] = v
            ordered[pl.ds(pl.multiple_of(g * part + b * BLOCK, BLOCK), BLOCK), :] = v
    tall = panel.shape[0] // HALVES
    for h in range(HALVES):
        outs[n + h][...] = ordered[h * tall : (h + 1) * tall, :]


def normalize(n, listed, panel, unit):
    rows, width = panel.shape
    part = rows // n
    shapes = [jax.ShapeDtypeStruct((part, width), jnp.bfloat16)] * n + [
        jax.ShapeDtypeStruct((rows // HALVES, width), jnp.bfloat16)
    ] * HALVES
    return pl.pallas_call(
        functools.partial(normalize_kernel, n),
        out_shape=shapes,
        in_specs=[whole(pltpu.HBM)] * 3,
        out_specs=[whole(VMEM)] * (n + HALVES),
        scratch_shapes=[
            pltpu.VMEM((n, part, width), jnp.bfloat16),
            pltpu.VMEM((width, width), jnp.bfloat16),
            pltpu.SMEM((1, listed.shape[1]), jnp.int32),
            pltpu.VMEM((rows, width), jnp.bfloat16),
            pltpu.SemaphoreType.DMA((n + 2,)),
        ],
        compiler_params=pltpu.CompilerParams(vmem_limit_bytes=LIMIT),
        cost_estimate=pl.CostEstimate(flops=2 * rows * width * width, bytes_accessed=6 * rows * width, transcendentals=0),
        name="normalize",
    )(listed, panel, unit)


def load_kernel(tile, out, came):
    x = pltpu.make_async_copy(tile, out, came)
    x.start()
    x.wait()


def load(tile):
    return pl.pallas_call(
        load_kernel,
        out_shape=jax.ShapeDtypeStruct(tile.shape, tile.dtype),
        in_specs=[whole(pltpu.HBM)],
        out_specs=whole(VMEM),
        scratch_shapes=[pltpu.SemaphoreType.DMA],
        compiler_params=pltpu.CompilerParams(vmem_limit_bytes=LIMIT),
        cost_estimate=pl.CostEstimate(flops=0, bytes_accessed=4 * tile.shape[0] * tile.shape[1], transcendentals=0),
        name="load",
    )(tile)


def pick_kernel(n, q, *refs):
    ins, outs = refs[:n], refs[n:]
    at = lax.axis_index("prow") ^ (lax.axis_index("pcol") // q)
    for b in range(n):

        @pl.when(at == b)
        def _():
            for m in range(n):
                outs[m][...] = ins[b ^ m][...]


def pick(n, q, pieces):
    shape = pieces[0].shape
    return pl.pallas_call(
        functools.partial(pick_kernel, n, q),
        out_shape=[jax.ShapeDtypeStruct(shape, jnp.bfloat16)] * n,
        in_specs=[whole(VMEM)] * n,
        out_specs=[whole(VMEM)] * n,
        compiler_params=pltpu.CompilerParams(vmem_limit_bytes=LIMIT),
        cost_estimate=pl.CostEstimate(flops=0, bytes_accessed=4 * n * shape[0] * shape[1], transcendentals=0),
        name="pick",
    )(*pieces)


def partial_kernel(n, q, halves, step, *refs):
    ins, tiles = refs[:n], refs[n : n + q]
    outs, held = refs[n + q : -1], refs[-1]
    p = lax.axis_index("prow")
    core = lax.axis_index("pcol") % q
    chunks, part, width = ins[0].shape
    for a in range(n):
        for k in range(chunks):
            held[pl.ds(pl.multiple_of((a ^ p) * part, part), part), k * width : (k + 1) * width] = ins[a][k]
    rows, depth = tiles[0].shape
    tall = rows // HALVES
    for i, h in enumerate(halves):
        for r in range(tall // step):
            base = h * tall + r * step
            total = None
            for e in range(q):
                right = held[pl.ds(pl.multiple_of((core ^ e) * depth, depth), depth), :]
                term = jnp.dot(tiles[e][base : base + step, :], right, preferred_element_type=jnp.float32)
                total = term if total is None else total + term
            for k in range(chunks):
                outs[k * len(halves) + i][r * step : (r + 1) * step, :] = total[:, k * width : (k + 1) * width].astype(
                    jnp.bfloat16
                )


def partial_product(n, q, halves, pieces, tiles):
    chunks, part, width = pieces[0].shape
    rows, depth = tiles[0].shape
    tall = rows // HALVES
    outs = pl.pallas_call(
        functools.partial(partial_kernel, n, q, halves, min(tall, 512)),
        out_shape=[jax.ShapeDtypeStruct((tall, width), jnp.bfloat16)] * (chunks * len(halves)),
        in_specs=[whole(VMEM)] * (n + q),
        out_specs=[whole(VMEM)] * (chunks * len(halves)),
        scratch_shapes=[pltpu.VMEM((n * part, chunks * width), jnp.bfloat16)],
        compiler_params=pltpu.CompilerParams(vmem_limit_bytes=LIMIT),
        cost_estimate=pl.CostEstimate(
            flops=2 * tall * len(halves) * width * chunks * depth * q,
            bytes_accessed=2 * q * tall * len(halves) * depth,
            transcendentals=0,
        ),
        name="partial_product",
    )(*pieces, *tiles)
    return [list(outs[k * len(halves) : (k + 1) * len(halves)]) for k in range(chunks)]


def piece_kernel(n, q, which, base, step, *refs):
    ins, tiles = refs[: len(which)], refs[len(which) : len(which) + q]
    before, out = refs[len(which) + q : -1], refs[-1]
    p = lax.axis_index("prow")
    core = lax.axis_index("pcol") % q
    _, part, _ = ins[0].shape
    each = n // q
    for r in range(out.shape[0] // step):
        here = slice(r * step, (r + 1) * step)
        there = slice(base + r * step, base + (r + 1) * step)
        total = before[0][there, :] if before else None
        for a, piece in zip(which, ins):
            g = a ^ p
            columns = pl.ds(pl.multiple_of((g % each) * part, part), part)
            left = tiles[0][there, columns]
            for e in range(1, q):
                left = jnp.where((core ^ e) == g // each, tiles[e][there, columns], left)
            term = jnp.dot(left, piece[0], preferred_element_type=jnp.float32)
            total = term if total is None else total + term
        out[here, :] = total.astype(out.dtype)


def piece_product(n, q, which, pieces, tiles, base, tall, before, dtype):
    _, part, width = pieces[0].shape
    return pl.pallas_call(
        functools.partial(piece_kernel, n, q, which, base, min(tall, 512)),
        out_shape=jax.ShapeDtypeStruct((tall, width), dtype),
        in_specs=[whole(VMEM)] * (len(which) + q + len(before)),
        out_specs=whole(VMEM),
        compiler_params=pltpu.CompilerParams(vmem_limit_bytes=LIMIT),
        cost_estimate=pl.CostEstimate(
            flops=2 * tall * width * part * len(which), bytes_accessed=2 * tall * part * len(which), transcendentals=0
        ),
        name="piece_product",
    )(*pieces, *tiles, *before)


def among(z, planes):
    return functools.reduce(jnp.logical_or, [z == y for y in planes])


def add_kernel(n, q, planes, x, y, out):
    z = lax.axis_index("pcol") // q
    total = x[...].astype(jnp.float32) + y[...].astype(jnp.float32)
    if len(planes) < n:
        total = jnp.where(among(z, planes), total, x[...].astype(jnp.float32))
    out[...] = total.astype(out.dtype)


def add(n, q, x, came):
    if came is None:
        return x
    y, planes = came
    return pl.pallas_call(
        functools.partial(add_kernel, n, q, planes),
        out_shape=jax.ShapeDtypeStruct(x.shape, x.dtype),
        in_specs=[whole(VMEM)] * 2,
        out_specs=whole(VMEM),
        compiler_params=pltpu.CompilerParams(vmem_limit_bytes=LIMIT),
        cost_estimate=pl.CostEstimate(flops=x.size, bytes_accessed=6 * x.size, transcendentals=0),
        name="add",
    )(x, y)


def ahead_kernel(*refs):
    count = len(refs) // 2
    loads, rows, out = refs[:count], refs[count:-1], refs[-1]
    tall = loads[0].shape[0]
    step = min(tall, 512)
    total = None
    for load, right in zip(loads, rows):
        for r in range(tall // step):
            here = slice(r * step, (r + 1) * step)
            left = load[here, :].astype(jnp.float32).T.astype(jnp.bfloat16)
            term = jnp.dot(left, right[here, :], preferred_element_type=jnp.float32)
            total = term if total is None else total + term
    out[...] = total.astype(out.dtype)


def ahead(loads, rows, dtype):
    tall, width = loads[0].shape
    return pl.pallas_call(
        ahead_kernel,
        out_shape=jax.ShapeDtypeStruct((width, width), dtype),
        in_specs=[whole(VMEM)] * (2 * len(loads)),
        out_specs=whole(VMEM),
        compiler_params=pltpu.CompilerParams(vmem_limit_bytes=LIMIT),
        cost_estimate=pl.CostEstimate(
            flops=2 * len(loads) * tall * width * width, bytes_accessed=4 * len(loads) * tall * width, transcendentals=0
        ),
        name="ahead",
    )(*loads, *rows)


def chosen_planes(n, q, planes):
    z = lax.axis_index("pcol") // q
    return [None if len(at) == n else among(z, at) for at in planes]


def gathered_kernel(n, q, planes, own, lhat, *refs):
    count = len(planes)
    early, came, total, sent = refs[:count], refs[count : 2 * count], refs[-2], refs[-1]
    takes = chosen_planes(n, q, planes)
    sum_ = own[...]
    for y, take in zip(early, takes):
        y = y[...].astype(jnp.float32)
        sum_ = sum_ + (y if take is None else jnp.where(take, y, 0.0))
    tall = lhat.shape[0]
    step = min(tall, 512)
    for r in range(tall // step):
        here = slice(r * step, (r + 1) * step)
        x = None
        for y, take in zip(came, takes):
            y = y[here, :].astype(jnp.float32)
            y = y if take is None else jnp.where(take, y, 0.0)
            x = y if x is None else x + y
        x = x.T
        high = x.astype(jnp.bfloat16)
        low = (x - high.astype(jnp.float32)).astype(jnp.bfloat16)
        sum_ = sum_ + jnp.dot(high, lhat[here, :], preferred_element_type=jnp.float32)
        sum_ = sum_ + jnp.dot(low, lhat[here, :], preferred_element_type=jnp.float32)
    total[...] = sum_
    sent[...] = sum_.astype(jnp.bfloat16)


def gathered(n, q, planes, own, lhat, early, came):
    tall, width = lhat.shape
    return pl.pallas_call(
        functools.partial(gathered_kernel, n, q, planes),
        out_shape=[jax.ShapeDtypeStruct(own.shape, jnp.float32), jax.ShapeDtypeStruct(own.shape, jnp.bfloat16)],
        in_specs=[whole(VMEM)] * (2 + len(early) + len(came)),
        out_specs=[whole(VMEM)] * 2,
        compiler_params=pltpu.CompilerParams(vmem_limit_bytes=LIMIT),
        cost_estimate=pl.CostEstimate(flops=4 * tall * width * width, bytes_accessed=6 * tall * width, transcendentals=0),
        name="gathered",
    )(own, lhat, *early, *came)


def masked_kernel(n, q, planes, rows, h, count, terms, listed, *refs):
    parts, off = refs[:count], refs[-2] if terms else refs[-1]
    if terms:
        pivot, *others = refs[count : count + terms]
        total = pivot[0]
        for y in others:
            total = total + y[...].astype(jnp.float32)
        refs[-1][0] = total
    p = lax.axis_index("prow")
    c = lax.axis_index("pcol")
    takes = chosen_planes(n, q, planes)
    per = off.shape[1] // BLOCK
    base = p * (rows // BLOCK) + (h * pl.num_programs(0) + pl.program_id(0)) * per
    x = parts[0][...].astype(jnp.float32)
    for y, take in zip(parts[1:], takes):
        y = y[...].astype(jnp.float32)
        x = x + (y if take is None else jnp.where(take, y, 0.0))
    x = x.T
    for b in range(per):
        keep = listed[c, base + b].astype(jnp.float32)
        off[:, b * BLOCK : (b + 1) * BLOCK] = -(x[:, b * BLOCK : (b + 1) * BLOCK] * keep)


def masked(n, q, planes, rows, h, listed, parts, before, terms=()):
    tall, width = parts[0].shape
    step = min(tall, 1024)
    count = tall // step
    return pl.pallas_call(
        functools.partial(masked_kernel, n, q, planes, rows, h, len(parts), len(terms)),
        grid=(count,),
        out_shape=[jax.ShapeDtypeStruct((width, rows), jnp.float32)]
        + [jax.ShapeDtypeStruct(x.shape, jnp.float32) for x in terms[:1]],
        in_specs=[whole(SMEM)]
        + [pl.BlockSpec((step, width), lambda i: (i, 0))] * len(parts)
        + [whole(VMEM)] * len(terms)
        + [whole(pl.ANY)] * len(before),
        out_specs=[pl.BlockSpec((width, step), lambda i: (0, h * count + i))] + [whole(VMEM)] * len(terms[:1]),
        input_output_aliases={1 + len(parts) + len(terms): 0} if before else {},
        compiler_params=pltpu.CompilerParams(vmem_limit_bytes=LIMIT),
        cost_estimate=pl.CostEstimate(flops=4 * tall * width, bytes_accessed=10 * tall * width, transcendentals=0),
        name="masked",
    )(listed, *parts, *terms, *before)


def per_device(n, ncol, l_panel, inverse_tile, unit_inverse, pivot_inverse, listed):
    return level(n, ncol, l_panel, inverse_tile, unit_inverse, pivot_inverse, listed)


def level(n, ncol, l_panel, inverse_tile, unit_inverse, pivot_inverse, listed):
    q = ncol // n
    devices = [(p, z, k) for p in range(n) for z in range(n) for k in range(q)]

    def at(p, z, k):
        return p * ncol + z * q + k

    def swap(x, move):
        pairs = []
        for d in devices:
            to = move(*d)
            if to is not None:
                pairs.append((at(*d), at(*to)))
        return lax.ppermute(x, AXES, pairs)

    def over_rows(x, a):
        return swap(x, lambda p, z, k: (p ^ a, z, k))

    made = normalize(n, *[pltpu.with_memory_space_constraint(x, pltpu.HBM) for x in (listed, l_panel, unit_inverse)])
    pieces, lhat = made[:n], made[n:]
    tiles = [load(inverse_tile)]
    tiles += [swap(inverse_tile, lambda p, z, k: (p, z, k ^ e)) for e in range(1, q)]
    tiles = [pltpu.with_memory_space_constraint(t, pltpu.VMEM) for t in tiles]

    def line_swap(x, odd, d):
        to = {}
        for z in line_pairs(n, d, odd):
            to[z], to[z + 1] = z + 1, z
        got = swap(x, lambda p, z, k: (p, to[z], k) if z in to else (p, z, k ^ (q > 1)))
        return got, tuple(sorted(to))

    sides = [odd for odd in (0, 1) if line_pairs(n, 1, odd)]
    theirs = {odd: line_swap(lhat[-1], odd, 1)[0] for odd in sides}

    scattered = [pieces[0]] + [over_rows(pieces[a], a) for a in range(1, n)]
    chosen = pick(n, q, scattered)

    mine = [chosen[0]] + [swap(chosen[m], lambda p, z, k: (p, z ^ m, k)) for m in range(1, n)]
    chunk = [None] * n
    for i, group in enumerate(groups(n)):
        load_ = jnp.stack([mine[m] for m in group])
        quarters = [load_] + [over_rows(load_, a) for a in range(1, n)]
        if i == 1:
            rows = inverse_tile.shape[0]
            most = piece_product(n, q, range(n - 1), quarters[:-1], tiles, 0, rows, [], jnp.float32)
            chunk[group[0]] = []
            for h in range(HALVES):
                tall = rows // HALVES
                x = piece_product(n, q, [n - 1], quarters[-1:], tiles, h * tall, tall, [most], jnp.bfloat16)
                chunk[group[0]].append(x)
        else:
            done = partial_product(n, q, tuple(range(HALVES)), quarters, tiles)
            for m, x in zip(group, done):
                chunk[m] = x

    z_here = lax.axis_index("pcol") // q

    def own(odd, d, h):
        at_mask = {}
        for z in range(n):
            to = z + d if (z % 2) == odd else z - d
            if 0 <= to < n:
                at_mask.setdefault(z ^ to, []).append(z)
        masks = sorted(at_mask)
        x = chunk[masks[0]][h]
        for m in masks[1:]:
            here = functools.reduce(jnp.logical_or, [z_here == z for z in at_mask[m]])
            x = jnp.where(here, chunk[m][h], x)
        return x

    early = []
    came = [[None, None] for _ in range(HALVES)]
    for d in range(n - 1, 0, -1):
        for h in range(HALVES):
            sent = [None, None]
            for odd in (0, 1):
                if not line_pairs(n, d, odd):
                    continue
                load_ = add(n, q, own(odd, d, h), came[h][1 - odd])
                sent[odd] = line_swap(load_, odd, d)
                if d == 1 and h == HALVES - 1:
                    term = ahead([load_], [theirs[odd]], jnp.bfloat16)
                    early.append(line_swap(term, odd, d)[0])
            came[h] = sent

    parts = [[chunk[0][h]] + [x[0] for x in came[h] if x is not None] for h in range(HALVES)]
    planes = [x[1] for x in came[0] if x is not None]
    part = ahead(chunk[0], lhat, jnp.float32)
    part, travel = gathered(n, q, planes, part, lhat[0], early, parts[0][1:])
    terms = [pivot_inverse, part] + [over_rows(travel, a) for a in range(1, n)]
    off = []
    for h in range(HALVES):
        last = h == HALVES - 1
        off = masked(n, q, planes, inverse_tile.shape[0], h, listed, parts[h], off[:1], terms if last else ())
    return off[0], off[1]


def groups(n):
    return [[0], [n - 1]] + [[m] for m in range(n - 2, 0, -1)]


def line_pairs(n, d, odd):
    return [z for z in range(odd, n - 1, 2) if z + d < n or z + 1 - d >= 0]


def solution(mesh):
    n, ncol = mesh.shape["prow"], mesh.shape["pcol"]
    return jax.shard_map(
        functools.partial(per_device, n, ncol),
        mesh=mesh,
        in_specs=(
            P("prow", "pcol"),
            P("prow", "pcol"),
            P("pcol", None, None),
            P("pcol", None, None),
            P(),
        ),
        out_specs=(P("pcol", "prow"), P("pcol", None, None)),
        check_vma=False,
    )
```
